32 devices in a mesh: group: 4 (over y, x), dp: 2 (over core), tensor: 4 (over z).
Axes of the slice: x: 2, y: 2, z: 4, core: 2. Of those that a mesh axis runs over, the one named last changes fastest.
Arguments:
- tokens: bfloat16 [8192, 2048], P(('group', 'dp')), may hold values from -6 to 6
- norm_gain: bfloat16 [2048], replicated, may hold values from 0.099609375 to 1.8984375
- w_query: bfloat16 [2048, 2048], P(None, 'tensor'), may hold values from -0.25 to 0.25
- w_keyval: bfloat16 [2048, 512], P(None, 'tensor'), may hold values from -0.125 to 0.125
- w_out: bfloat16 [2048, 2048], P('tensor'), may hold values from -0.8984375 to 0.8984375
- kv_cache: bfloat16 [4, 32, 16, 128, 512], P(None, ('group', 'dp'), None, None, 'tensor'), may hold values from -400 to 400
- lengths: int32 [32, 2], P(('group', 'dp')), may hold values from 0 to 2048, as said below
- dest_slot: int32 [32, 16], replicated, may hold values from 0 to 511, as said below
Outputs:
- mixed: bfloat16 [8192, 2048], P(('group', 'dp', 'tensor'))
- decode_cache: bfloat16 [4, 512, 128, 512], P(None, ('group', 'dp'), None, 'tensor')
The draws below stay inside these ranges and needn't reach their ends.
Inputs may be any that keep to these rules, and one draw needn't show every extreme that they name: lengths[p, 0] lies in 0 to 2048 and lengths[p, 1] in 1 to 256; 2048 and 256 are each taken by some prompt; the prompts r * 4 to r * 4 + 3 of each index r of group and dp together hold exactly 32 live blocks. dest_slot is a permutation of the 512 slots; the slots of the index r of group and dp together are r * 4 * 16 onward; the blocks of prompts r * 4 to r * 4 + 3 send exactly 8 blocks to each index, of which exactly 4 is live.
All inputs are finite; a program needn't handle non-finite values.
Results may differ from the reference program's by a relative error of at most 0.009.
Values may be sent and summed in bfloat16 or wider, within the bound.
A program may use at most 128 MiB of HBM per device.

```python
import jax
import jax.numpy as jnp
from jax import lax

D = 2048
H = 32
HD = 64
KVH = 4
BLK = 128
NBW = 16
NEW = 256
LAYERS = 4
PR_DEV = 4
WIN = 2048
PROMPTS = 32
TOKENS = 8192
N_GROUP = 4
N_DP = 2


def draw_kv_cache(key, part):
    shape = (LAYERS, PROMPTS, NBW, BLK, KVH * 2 * HD)
    normal_vals = jnp.clip(jax.random.normal(jax.random.fold_in(key, 3), shape, jnp.float32), -6.0, 6.0)
    return normal_vals.astype(jnp.bfloat16)


def live_plan(key):
    base = jax.random.fold_in(key, 7)
    half = PROMPTS // 2
    first = jax.random.randint(jax.random.fold_in(base, 1), (half,), 0, NBW + 1)
    top_pair = jax.random.randint(jax.random.fold_in(base, 3), (), 0, half)
    first = jnp.where(jnp.arange(half) == top_pair, NBW, first)
    counts = jnp.stack([first, NBW - first], axis=1).reshape(PROMPTS)
    offset = jax.random.randint(jax.random.fold_in(base, 5), (PROMPTS,), 0, BLK)
    history = jnp.where(counts > 0, (counts - 1) * BLK + 1 + offset, 0)
    history = jnp.where(jnp.arange(PROMPTS) == 2 * top_pair, WIN, history)
    return (counts.astype(jnp.int32), history.astype(jnp.int32))


def draw_lengths(key, part):
    counts, history = live_plan(key)
    base = jax.random.fold_in(key, 9)
    fresh_len = jax.random.randint(jax.random.fold_in(base, 2), (PROMPTS,), 1, NEW + 1)
    top_new = jax.random.randint(jax.random.fold_in(base, 4), (), 0, PROMPTS)
    fresh_len = jnp.where(jnp.arange(PROMPTS) == top_new, NEW, fresh_len)
    return jnp.stack([history, fresh_len], axis=1).astype(jnp.int32)


def draw_dest_slot(key, part):
    counts, history = live_plan(key)
    devices = N_GROUP * N_DP
    per_dev = PR_DEV * NBW
    per_peer = per_dev // devices
    live = (jnp.arange(NBW)[None, :] >= NBW - counts[:, None]).astype(jnp.int32).reshape(devices, per_dev)
    base = jax.random.fold_in(key, 11)
    mix_keys = jax.random.split(jax.random.fold_in(base, 3), devices)
    mix = jax.vmap(lambda kk: jax.random.permutation(kk, per_dev))(mix_keys)
    score = (1 - live) * per_dev + mix
    order = jnp.argsort(score, axis=1, stable=True)
    position = jnp.argsort(order, axis=1, stable=True)
    shifts = jax.random.randint(jax.random.fold_in(base, 4), (devices, 1), 0, devices)
    receiver = (position + shifts) % devices
    within = position // devices
    recv_keys = jax.random.split(jax.random.fold_in(base, 2), devices)
    recv_perm = jax.vmap(lambda kk: jax.random.permutation(kk, per_dev))(recv_keys)
    senders = jnp.arange(devices)[:, None]
    slot_local = recv_perm[receiver, senders * per_peer + within]
    dest = receiver * per_dev + slot_local
    return dest.reshape(PROMPTS, NBW).astype(jnp.int32)


def level_of(stream_key, shape, shards, least, largest):
    def one(axis_at, shards_of):
        draws = jax.random.uniform(jax.random.fold_in(jax.random.fold_in(stream_key, 6), axis_at), (shards_of,), jnp.float32, least / len(shards), largest / len(shards))
        return jnp.repeat(jnp.exp(draws), shape[axis_at] // shards_of).reshape((-1,) + (1,) * (len(shape) - axis_at - 1))

    level = one(*shards[0])
    for cut in shards[1:]:
        level = level * one(*cut)
    return level


def centred(rng, extent, width, reach, pieces=(), kind=jnp.bfloat16):
    values = jax.random.normal(rng, extent, jnp.float32) * width
    if len(pieces) > 0:
        values = level_of(rng, extent, pieces, -0.22, 0.18) * values
    return jnp.clip(values, min=-reach, max=reach).astype(kind)


def setup_inputs(seed: int = 0) -> dict:
    key_list = jax.random.split(jax.random.key(seed), 9)
    tokens = centred(key_list[0], (TOKENS, D), 1.0, 6.0, ((0, 8),))
    norm_gain = jnp.clip(1.0 + 0.18 * jax.random.normal(key_list[1], (D,), jnp.float32), 0.099609375, 1.8984375).astype(jnp.bfloat16)
    w_query = centred(key_list[2], (D, H * HD), (D // 4) ** -0.5, 0.25, ((1, 4),))
    w_keyval = centred(key_list[3], (D, KVH * 2 * HD), D ** -0.5, 0.125, ((1, 4),))
    w_out = centred(key_list[4], (H * HD, D), 0.15, 0.8984375, ((0, 4),))
    kv_cache = draw_kv_cache(jax.random.fold_in(key_list[8], 71), 0)
    lengths = draw_lengths(jax.random.fold_in(key_list[8], 71), 0)
    dest_slot = draw_dest_slot(jax.random.fold_in(key_list[8], 71), 0)
    return dict(tokens=tokens, norm_gain=norm_gain, w_query=w_query, w_keyval=w_keyval, w_out=w_out, kv_cache=kv_cache, lengths=lengths, dest_slot=dest_slot)


def reference(tokens, norm_gain, w_query, w_keyval, w_out, kv_cache, lengths, dest_slot):
    tokens_f = tokens.astype(jnp.float32)
    normed = (tokens_f * lax.rsqrt(lax.optimization_barrier(jnp.mean(tokens_f * tokens_f, axis=-1, keepdims=True)) + 1e-05) * norm_gain.astype(jnp.float32)).astype(jnp.bfloat16)
    query = jnp.dot(normed, w_query, preferred_element_type=jnp.float32).astype(jnp.bfloat16)
    query = query.reshape(PROMPTS, NEW, KVH, H // KVH, HD)
    keyval = jnp.dot(normed, w_keyval, preferred_element_type=jnp.float32).astype(jnp.bfloat16)
    keyval = keyval.reshape(PROMPTS, NEW, KVH, 2, HD)
    cache = kv_cache[0].reshape(PROMPTS, WIN, KVH, 2, HD)
    scale = 1.0 / HD ** 0.5
    query_pos = jnp.arange(NEW)[:, None]
    key_pos = jnp.arange(WIN + NEW)[None, :]

    def attend(items):
        query_p, cache_p, fresh_p, history, fresh_len = items
        pairs = jnp.concatenate([cache_p, fresh_p], axis=0)
        keys_f = pairs[:, :, 0].astype(jnp.float32)
        vals_f = pairs[:, :, 1].astype(jnp.float32)
        scores = jnp.einsum('ckgd,tkd->kgct', query_p.astype(jnp.float32), keys_f) * scale
        visible = jnp.where(key_pos < WIN, (key_pos >= WIN - history) & (key_pos >= query_pos + 1), key_pos - WIN <= query_pos)
        scores = jnp.where(visible, scores, -1e+30)
        scores = scores - lax.optimization_barrier(jnp.max(scores, axis=-1, keepdims=True))
        expo = jnp.exp(scores)
        weights = (expo / lax.optimization_barrier(jnp.sum(expo, axis=-1, keepdims=True))).astype(jnp.bfloat16)
        mixed_p = jnp.einsum('kgct,tkd->ckgd', weights.astype(jnp.float32), vals_f)
        mixed_p = mixed_p.astype(jnp.bfloat16).reshape(NEW, H * HD)
        return jnp.where((jnp.arange(NEW) < fresh_len)[:, None], mixed_p, jnp.zeros_like(mixed_p))
    attn = lax.map(attend, (query, cache, keyval, lengths[:, 0], lengths[:, 1]))
    attn = attn.reshape(TOKENS, H * HD)
    mixed = jnp.dot(attn, w_out, preferred_element_type=jnp.float32).astype(jnp.bfloat16)
    live_mask = ((jnp.arange(NBW)[None, :] + 1) * BLK > WIN - lengths[:, 0:1]).astype(kv_cache.dtype)
    blocks = kv_cache * live_mask[None, :, :, None, None]
    blocks = blocks.reshape(LAYERS, PROMPTS * NBW, BLK, KVH * 2 * HD)
    decode_cache = jnp.zeros_like(blocks).at[:, dest_slot.reshape(-1).astype(jnp.int32)].set(blocks)
    return (mixed, decode_cache)
```

```python
import functools

import jax
import jax.numpy as jnp
from jax import lax
from jax.experimental import pallas as pl
from jax.experimental.pallas import tpu as pltpu
from jax.sharding import PartitionSpec as P

HD = 64
EPS = 1e-05
NEG = -1e30
FAR = -(1 << 20)
VMEM_LIMIT = 60 * 1024 * 1024
MESH = pl.DeviceIdType.MESH
GROUP_HEADS = 4
CORES = 2

PROMPT, KEY0, KEY1, POS0, POS1, FIRST, LAST = range(7)


def plan_kernel(dest_ref, len_ref, order_ref, plan_ref, slot_ref, count_ref):
    blocks, all_prompts = dest_ref.shape
    prompts = len_ref.shape[1]
    per_dev = prompts * blocks
    devices = slot_ref.shape[0]
    cap = order_ref.shape[0] // devices
    steps = plan_ref.shape[1]
    me = lax.axis_index("group") * lax.axis_size("dp") + lax.axis_index("dp")
    block_len = 128
    window = blocks * block_len

    def clear(i, carry):
        count_ref[i] = 0
        return carry

    lax.fori_loop(0, devices, clear, 0)

    def first_block(p):
        return (window - len_ref[0, p]) // block_len

    def emit(n, p, k0, k1, at0, at1, new):
        plan_ref[PROMPT, n] = p
        plan_ref[KEY0, n] = k0
        plan_ref[KEY1, n] = k1
        plan_ref[POS0, n] = at0
        plan_ref[POS1, n] = at1
        plan_ref[FIRST, n] = new

    def prompt(p, n):
        begin = first_block(p)

        def block(b, carry):
            dest = dest_ref[b, me * prompts + p]
            peer = dest // per_dev
            k = peer * cap + count_ref[peer]
            count_ref[peer] = count_ref[peer] + 1
            order_ref[k] = p * blocks + b
            slot_ref[peer, pl.ds(k - peer * cap, 1), :] = jnp.full(
                (1, 128), dest - peer * per_dev, jnp.int32
            )
            return carry

        lax.fori_loop(begin, blocks, block, 0)
        fresh = per_dev + 2 * p
        emit(n, p, fresh, fresh + 1, 0, block_len, 1)
        pairs = (blocks - begin + 1) // 2

        def pair(i, carry):
            b = begin + 2 * i
            at = p * blocks + b
            second = b + 1 < blocks
            pos = b * block_len - window
            emit(
                n + 1 + i,
                p,
                at,
                jnp.where(second, at + 1, at),
                pos,
                jnp.where(second, pos + block_len, FAR),
                0,
            )
            return carry

        lax.fori_loop(0, pairs, pair, 0)
        plan_ref[LAST, p] = n + pairs
        return n + 1 + pairs

    n = lax.fori_loop(0, prompts, prompt, 0)

    def pad(i, carry):
        emit(i, 0, 0, 0, FAR, FAR, 1)
        return carry

    lax.fori_loop(n, steps, pad, 0)


def main_kernel(
    sizes,
    order_ref,
    plan_ref,
    len_ref,
    slot_ref,
    gain_ref,
    tok_hbm,
    wq_hbm,
    wkv_hbm,
    wout_hbm,
    cache_hbm,
    mixed_ref,
    land_ref,
    slot_out,
    tok,
    wq,
    wkv,
    kvb,
    *scratch,
):
    layers = land_ref.shape[0]
    caches = (kvb,) + scratch[: layers - 1]
    run(
        sizes,
        (order_ref, plan_ref, len_ref, slot_ref, gain_ref),
        (tok_hbm, wq_hbm, wkv_hbm, wout_hbm, cache_hbm),
        (mixed_ref, land_ref, slot_out),
        (tok, wq, wkv, kvb, caches),
        *scratch[layers - 1 :],
    )


def run(
    sizes,
    scalars,
    args,
    outs,
    bufs,
    pack,
    wall,
    q_ref,
    acc_ref,
    m_ref,
    attn,
    attn_in,
    total_ref,
    load_sem,
    own_sem,
    z1_send,
    z1_recv,
    z2_send,
    z2_recv,
    xy_send,
    xy_recv,
    s1_send,
    s1_recv,
    s2_send,
    s2_recv,
    hand_send,
    hand_recv,
    slot_send,
    slot_recv,
    at_send,
    at_recv,
):
    order_ref, plan_ref, len_ref, slot_ref, gain_ref = scalars
    tok_hbm, wq_hbm, wkv_hbm, wout_hbm, cache_hbm = args
    mixed_ref, land_ref, slot_out = outs
    tok, wq, wkv, kvb, caches = bufs
    G, DP, T = sizes
    R = G * DP
    g, d, t = lax.axis_index("group"), lax.axis_index("dp"), lax.axis_index("tensor")
    r = g * DP + d
    core = d % CORES
    sib = d + 1 - 2 * core
    layers = land_ref.shape[0]
    cap = land_ref.shape[1] // R
    per_dev = cache_hbm.shape[1]
    prompts, rows, width = tok.shape
    groups, _, qrows, lanes = q_ref.shape
    heads = qrows // rows
    steps = plan_ref.shape[1]
    half = wall.shape[1] // CORES
    rest = half - R1_ROWS
    quarter = rest // G

    def load(i, src, dst):
        return pltpu.make_async_copy(src, dst, load_sem.at[i])

    loads = (
        [load(0, cache_hbm.at[0], kvb.at[pl.ds(0, per_dev)])]
        + [load(l, cache_hbm.at[l], caches[l]) for l in range(1, layers)]
        + [
            load(layers, tok_hbm, tok),
            load(layers + 1, wkv_hbm, wkv),
            load(layers + 2, wq_hbm, wq),
            load(layers + 3, wout_hbm, wall.at[t]),
        ]
    )
    for c in loads:
        c.start()

    def remote(src, dst, send, recv, dev):
        return pltpu.make_async_remote_copy(
            src_ref=src, dst_ref=dst, send_sem=send, recv_sem=recv, device_id=dev, device_id_type=MESH
        )

    barrier = pltpu.get_barrier_semaphore()

    def hello(e, carry):
        to = r ^ e
        pl.semaphore_signal(barrier, 1, device_id=(to // DP, to % DP, t), device_id_type=MESH)
        return carry

    lax.fori_loop(1, R, hello, 0)
    for k in range(1, T):
        pl.semaphore_signal(barrier, 1, device_id=(g, d, (t + k) % T), device_id_type=MESH)
    pl.semaphore_wait(barrier, R - 1 + T - 1)

    mine1 = pl.ds(pl.multiple_of(core * half, 16), R1_ROWS)
    mine2 = pl.ds(pl.multiple_of(core * half + R1_ROWS, 16), rest)
    mine2q = pl.ds(pl.multiple_of(core * half + R1_ROWS + g * quarter, 16), quarter)

    def z1(k):
        return remote(
            wout_hbm.at[mine1], wall.at[t, mine1], z1_send.at[k - 1], z1_recv.at[k - 1], (g, d, (t + k) % T)
        )

    def z1_direct(k):
        to = (t + k) % T
        return abs(to - t) < T - 1

    def z2(k):
        return remote(
            wout_hbm.at[mine2q], wall.at[t, mine2q], z2_send.at[k - 1], z2_recv.at[k - 1], (g, d, (t + k) % T)
        )

    def origin(k):
        return (t + T - k) % T

    def xy(k, e):
        part = wall.at[origin(k), mine2q]
        i = (k - 1) * (G - 1) + e - 1
        return remote(part, part, xy_send.at[i], xy_recv.at[i], (g ^ e, d, t))

    def s1(k):
        part = wall.at[origin(k), mine1]
        return remote(part, part, s1_send.at[k - 1], s1_recv.at[k - 1], (g, sib, t))

    def s2(k):
        part = wall.at[origin(k), mine2]
        return remote(part, part, s2_send.at[k - 1], s2_recv.at[k - 1], (g, sib, t))

    def forward():
        part = wall.at[origin(T - 2), mine1]
        to = jnp.where(t == 1, 0, T - 1)
        k = jnp.where(t == 1, 1, T - 1)
        return remote(part, part, z1_send.at[T - 1], z1_recv.at[k - 1], (g, d, to))

    def hand(l, e):
        to = r ^ e
        return remote(
            pack.at[l, pl.ds(to * cap, cap)],
            land_ref.at[l, pl.ds(r * cap, cap)],
            hand_send.at[l, e],
            hand_recv.at[l, e],
            (to // DP, to % DP, t),
        )

    def slots(e):
        to = r ^ e
        return remote(
            slot_ref.at[to], slot_out.at[r], slot_send.at[e], slot_recv.at[e], (to // DP, to % DP, t)
        )

    def exchange(n, k):
        i = n * (T - 1) + k - 1
        pairs = heads // 2
        to = (t + k) % T
        return remote(
            attn.at[to, pl.ds(n * pairs, pairs)],
            attn_in.at[t, pl.ds(n * pairs, pairs)],
            at_send.at[i],
            at_recv.at[i],
            (g, d, to),
        )

    for k in range(1, T):
        z2(k).start()
    for k in range(1, T):
        pl.when(z1_direct(k))(z1(k).start)

    def hello_slots(e, carry):
        slots(e).start()
        return carry

    lax.fori_loop(1, R, hello_slots, 0)
    own_slots = pltpu.make_async_copy(slot_ref.at[r], slot_out.at[r], own_sem.at[layers])
    own_slots.start()

    def own(l):
        span = pl.ds(r * cap, cap)
        return pltpu.make_async_copy(pack.at[l, span], land_ref.at[l, span], own_sem.at[l])

    for l in range(layers):
        loads[l].wait()

        def put(i, carry):
            pack[l, i] = caches[l][order_ref[i]]
            return carry

        lax.fori_loop(0, R * cap, put, 0)

        def send(e, carry):
            hand(l, e).start()
            return carry

        lax.fori_loop(1, R, send, 0)
        own(l).start()

    loads[layers].wait()
    loads[layers + 1].wait()
    loads[layers + 2].wait()
    low = lax.broadcasted_iota(jnp.int32, (rows, lanes), 1) < HD

    def project(p, carry):
        x = tok[p].astype(jnp.float32)
        inv = lax.rsqrt(jnp.mean(x * x, axis=-1, keepdims=True) + EPS)
        normed = (x * inv * gain_ref[...].astype(jnp.float32)).astype(jnp.bfloat16)
        kv = jnp.dot(normed, wkv[...], preferred_element_type=jnp.float32).astype(jnp.bfloat16)
        kvb[pl.ds(per_dev + 2 * p, 2)] = kv.reshape(2, rows // 2, lanes)
        q = jnp.dot(normed, wq[...], preferred_element_type=jnp.float32) * (1.0 / HD**0.5)
        for pair in range(q.shape[1] // lanes):
            both = q[:, pair * lanes : (pair + 1) * lanes]
            n, at = (2 * pair) // heads, (2 * pair) % heads
            q_ref[n, p, at * rows : (at + 1) * rows] = jnp.where(low, both, 0.0).astype(jnp.bfloat16)
            q_ref[n, p, (at + 1) * rows : (at + 2) * rows] = jnp.where(
                low, pltpu.roll(both, HD, 1), 0.0
            ).astype(jnp.bfloat16)
        return carry

    lax.fori_loop(0, prompts, project, 0)

    for k in range(1, T):
        z2(k).wait_recv()
        for e in range(1, G):
            xy(k, e).start()

    trans = (((1,), (1,)), ((), ()))
    keys = 2 * kvb.shape[1]
    row = lax.broadcasted_iota(jnp.int32, (rows, keys), 0)
    col = lax.broadcasted_iota(jnp.int32, (1, keys), 1)
    key_low = lax.broadcasted_iota(jnp.int32, (keys, lanes), 1) < HD
    window = per_dev // prompts * kvb.shape[1]
    acc_ref[0] = jnp.zeros(acc_ref.shape[1:], acc_ref.dtype)
    m_ref[...] = jnp.full(m_ref.shape, NEG, m_ref.dtype)

    def attend(n):
        def step(i, carry):
            p = plan_ref[PROMPT, i]
            kv = jnp.concatenate([kvb[plan_ref[KEY0, i]], kvb[plan_ref[KEY1, i]]], axis=0)
            ones = jnp.where(key_low, jnp.ones_like(kv), kv)
            at = jnp.where(
                col < keys // 2, plan_ref[POS0, i] + col, plan_ref[POS1, i] + (col - keys // 2)
            )
            seen = (at <= row) & (at >= jnp.maximum(row + (1 - window), -len_ref[0, p]))
            for h in range(heads):
                s = lax.dot_general(
                    q_ref[n, p, h * rows : (h + 1) * rows], kv, trans, preferred_element_type=jnp.float32
                )
                s = jnp.where(seen, s, NEG)
                before = jnp.where(plan_ref[FIRST, i] == 1, NEG, m_ref[h])
                best = jnp.maximum(s[:, :lanes], s[:, lanes:])
                m = jnp.maximum(before, jnp.max(best, axis=1, keepdims=True))
                e = jnp.exp(s - jnp.concatenate([m, m], axis=1))
                o = jnp.dot(e.astype(jnp.bfloat16), ones, preferred_element_type=jnp.float32)
                acc_ref[i + 1, h] = acc_ref[i, h] * jnp.exp(before - m) + o
                m_ref[h] = m
            return carry

        lax.fori_loop(0, steps, step, 0)

        def finish(p, carry):
            live = lax.broadcasted_iota(jnp.int32, (rows, lanes), 0) < len_ref[1, p]
            end = plan_ref[LAST, p] + 1
            for pair in range(heads // 2):
                even, odd = acc_ref[end, 2 * pair], acc_ref[end, 2 * pair + 1]
                num = jnp.where(low, pltpu.roll(even, HD, 1), odd)
                den = jnp.where(low, even, pltpu.roll(odd, HD, 1))
                attn[p, n * (heads // 2) + pair] = jnp.where(live, num / den, 0.0).astype(jnp.bfloat16)
            return carry

        lax.fori_loop(0, prompts, finish, 0)
        for k in range(1, T):
            exchange(n, k).start()

    ends = (t == 1) | (t == T - 2)
    for n in range(groups):
        attend(n)
        if n == 0:
            z1(T - 2).wait_recv()
            pl.when(ends)(lambda: forward().start())
            s1(T - 2).start()
            for k in (1, T - 1):

                @pl.when(abs(origin(k) - t) < T - 1)
                def _():
                    z1(k).wait_recv()
                    s1(k).start()

    for k in range(1, T):
        for e in range(1, G):
            xy(k, e).wait_recv()
        s2(k).start()

    def mix(part, o, begin):
        a = jnp.concatenate([part[i] for i in range(part.shape[0])], axis=1)

        def tile(j, carry):
            at = pl.ds(pl.multiple_of(j * total_ref.shape[2], 128), total_ref.shape[2])
            term = jnp.dot(a, wall[o, :, at], preferred_element_type=jnp.float32)
            total_ref[j] = term if begin else total_ref[j] + term
            return carry

        lax.fori_loop(0, total_ref.shape[0], tile, 0)

    loads[layers + 3].wait()
    mix(attn.at[t], t, True)
    for k in (1, T - 1):

        @pl.when(abs(origin(k) - t) == T - 1)
        def _():
            z1(k).wait_recv()
            s1(k).start()

    for k in (2, 1, 3):
        s1(k).wait_recv()
        s2(k).wait_recv()
        for n in range(groups):
            exchange(n, k).wait_recv()
        mix(attn_in.at[origin(k)], origin(k), False)
    for j in range(total_ref.shape[0]):
        w = total_ref.shape[2]
        mixed_ref[:, j * w : (j + 1) * w] = total_ref[j].astype(jnp.bfloat16)

    for k in range(1, T):
        z2(k).wait_send()
        pl.when(z1_direct(k))(z1(k).wait_send)
        s1(k).wait_send()
        s2(k).wait_send()
        for e in range(1, G):
            xy(k, e).wait_send()
        for n in range(groups):
            exchange(n, k).wait_send()
    pl.when(ends)(lambda: forward().wait_send())
    own_slots.wait()

    def done(e, carry):
        slots(e).wait()
        for l in range(layers):
            hand(l, e).wait()
        return carry

    lax.fori_loop(1, R, done, 0)
    for l in range(layers):
        own(l).wait()


R1_ROWS = 128


def place_kernel(slot_ref, land_ref, out_ref, src_ref, zero_ref, sems):
    layers, slots, block_len, _ = out_ref.shape
    devices = slot_ref.shape[0]
    total = land_ref.shape[1]
    cap = total // devices
    zero_ref[...] = jnp.zeros_like(zero_ref)

    def clear(j, carry):
        src_ref[j] = -1
        return carry

    lax.fori_loop(0, slots, clear, 0)

    def send(j, carry):
        slot = slot_ref[j // cap, j % cap, 0]
        src_ref[slot] = j
        pltpu.make_async_copy(land_ref.at[:, j], out_ref.at[:, slot], sems.at[slot]).start()
        return carry

    lax.fori_loop(0, total, send, 0)

    def fill(j, carry):
        @pl.when(src_ref[j] < 0)
        def _():
            pltpu.make_async_copy(zero_ref, out_ref.at[:, j], sems.at[j]).start()

        return carry

    lax.fori_loop(0, slots, fill, 0)

    def done(j, carry):
        pltpu.make_async_copy(zero_ref, out_ref.at[:, j], sems.at[j]).wait()
        return carry

    lax.fori_loop(0, slots, done, 0)


def per_device(tokens, norm_gain, w_query, w_keyval, w_out, kv_cache, lengths, dest_slot):
    prompts = lengths.shape[0]
    all_rows, width = tokens.shape
    rows = all_rows // prompts
    layers, _, blocks_win, block_len, lanes = kv_cache.shape
    per_dev = prompts * blocks_win
    G, DP, T = lax.axis_size("group"), lax.axis_size("dp"), lax.axis_size("tensor")
    R = G * DP
    cap = per_dev // R // 2
    live = R * cap
    steps = prompts + (live + prompts) // 2
    heads = w_query.shape[1] // HD
    groups = heads // GROUP_HEADS
    bf, f32 = jnp.bfloat16, jnp.float32

    smem = pl.BlockSpec(memory_space=pltpu.SMEM)
    hbm = pl.BlockSpec(memory_space=pltpu.HBM)
    vmem = pl.BlockSpec(memory_space=pltpu.VMEM)
    dest_t, len_t = dest_slot.T, lengths.T
    order, plan, slots = pl.pallas_call(
        plan_kernel,
        in_specs=[smem, smem],
        out_specs=[smem, smem, vmem],
        out_shape=[
            jax.ShapeDtypeStruct((live,), jnp.int32),
            jax.ShapeDtypeStruct((7, steps), jnp.int32),
            jax.ShapeDtypeStruct((R, 8, 128), jnp.int32),
        ],
        scratch_shapes=[pltpu.SMEM((R,), jnp.int32)],
        name="plan",
    )(dest_t, len_t)

    sem = pltpu.SemaphoreType.DMA
    depth = w_out.shape[0]
    mixed, landed, slots_in = pl.pallas_call(
        functools.partial(main_kernel, (G, DP, T)),
        in_specs=[smem, smem, smem, vmem, vmem] + [hbm] * 5,
        out_specs=[vmem, hbm, vmem],
        out_shape=[
            jax.ShapeDtypeStruct((rows, width), bf),
            jax.ShapeDtypeStruct((layers, live, block_len, lanes), bf),
            jax.ShapeDtypeStruct((R, 8, 128), jnp.int32),
        ],
        scratch_shapes=[
            pltpu.VMEM((prompts, rows, width), bf),
            pltpu.VMEM(w_query.shape, bf),
            pltpu.VMEM(w_keyval.shape, bf),
            pltpu.VMEM((per_dev + 2 * prompts, block_len, lanes), bf),
            *[pltpu.VMEM((per_dev, block_len, lanes), bf) for _ in range(layers - 1)],
            pltpu.VMEM((layers, live, block_len, lanes), bf),
            pltpu.VMEM((T, depth, width), bf),
            pltpu.VMEM((groups, prompts, GROUP_HEADS * rows, lanes), bf),
            pltpu.VMEM((steps + 1, GROUP_HEADS, rows, lanes), f32),
            pltpu.VMEM((GROUP_HEADS, rows, lanes), f32),
            pltpu.VMEM((prompts, heads // 2, rows, lanes), bf),
            pltpu.VMEM((T, heads // 2, rows, lanes), bf),
            pltpu.VMEM((4, rows, width // 4), f32),
            sem((layers + 4,)),
            sem((layers + 1,)),
            sem((T,)),
            sem((T - 1,)),
            sem((T - 1,)),
            sem((T - 1,)),
            sem(((T - 1) * (G - 1),)),
            sem(((T - 1) * (G - 1),)),
            sem((T - 1,)),
            sem((T - 1,)),
            sem((T - 1,)),
            sem((T - 1,)),
            sem((layers, R)),
            sem((layers, R)),
            sem((R,)),
            sem((R,)),
            sem((groups * (T - 1),)),
            sem((groups * (T - 1),)),
        ],
        compiler_params=pltpu.CompilerParams(
            collective_id=0, has_side_effects=True, vmem_limit_bytes=VMEM_LIMIT
        ),
        name="main",
    )(
        order,
        plan,
        len_t,
        slots,
        norm_gain.reshape(1, width),
        tokens.reshape(prompts, rows, width),
        w_query,
        w_keyval,
        w_out,
        kv_cache.reshape(layers, per_dev, block_len, lanes),
    )

    decode_cache = pl.pallas_call(
        place_kernel,
        in_specs=[smem, hbm],
        out_specs=hbm,
        out_shape=jax.ShapeDtypeStruct((layers, per_dev, block_len, lanes), bf),
        scratch_shapes=[
            pltpu.SMEM((per_dev,), jnp.int32),
            pltpu.VMEM((layers, block_len, lanes), bf),
            sem((per_dev,)),
        ],
        name="place",
    )(slots_in, landed)
    return (mixed, decode_cache)


def solution(mesh):
    in_specs = (
        P(("group", "dp"), None),
        P(),
        P(None, "tensor"),
        P(None, "tensor"),
        P("tensor", None),
        P(None, ("group", "dp"), None, None, "tensor"),
        P(("group", "dp"), None),
        P(),
    )
    out_specs = (P(("group", "dp", "tensor"), None), P(None, ("group", "dp"), None, "tensor"))
    return jax.shard_map(
        per_device, mesh=mesh, in_specs=in_specs, out_specs=out_specs, check_vma=False
    )
```

```python
import functools

import jax
import jax.numpy as jnp
from jax import lax
from jax.experimental import pallas as pl
from jax.experimental.pallas import tpu as pltpu
from jax.sharding import PartitionSpec as P

HD = 64
EPS = 1e-05
NEG = -1e30
FAR = -(1 << 20)
VMEM_LIMIT = 60 * 1024 * 1024
MESH = pl.DeviceIdType.MESH
GROUP_HEADS = 4
CORES = 2

PROMPT, KEY0, KEY1, POS0, POS1, FIRST, LAST = range(7)


def plan_kernel(
    dest_ref, len_ref, order_ref, plan_ref, slot_ref, blank_ref, count_ref, zero_ref, sems
):
    span = zero_ref.shape[0]
    layers, slots = blank_ref.shape[:2]
    zero_ref[...] = jnp.zeros_like(zero_ref)
    fills = [
        pltpu.make_async_copy(zero_ref, blank_ref.at[l, pl.ds(i * span, span)], sems.at[l, i])
        for l in range(layers)
        for i in range(slots // span)
    ]
    for c in fills:
        c.start()
    blocks, all_prompts = dest_ref.shape
    prompts = len_ref.shape[1]
    per_dev = prompts * blocks
    devices = slot_ref.shape[0]
    cap = order_ref.shape[0] // devices
    steps = plan_ref.shape[1]
    me = lax.axis_index("group") * lax.axis_size("dp") + lax.axis_index("dp")
    block_len = 128
    window = blocks * block_len

    def clear(i, carry):
        count_ref[i] = 0
        return carry

    lax.fori_loop(0, devices, clear, 0)

    def first_block(p):
        return (window - len_ref[0, p]) // block_len

    def emit(n, p, k0, k1, at0, at1, new):
        plan_ref[PROMPT, n] = p
        plan_ref[KEY0, n] = k0
        plan_ref[KEY1, n] = k1
        plan_ref[POS0, n] = at0
        plan_ref[POS1, n] = at1
        plan_ref[FIRST, n] = new

    def prompt(p, n):
        begin = first_block(p)

        def block(b, carry):
            dest = dest_ref[b, me * prompts + p]
            peer = dest // per_dev
            k = peer * cap + count_ref[peer]
            count_ref[peer] = count_ref[peer] + 1
            order_ref[k] = p * blocks + b
            slot_ref[peer, pl.ds(k - peer * cap, 1), :] = jnp.full(
                (1, 128), dest - peer * per_dev, jnp.int32
            )
            return carry

        lax.fori_loop(begin, blocks, block, 0)
        fresh = per_dev + 2 * p
        emit(n, p, fresh, fresh + 1, 0, block_len, 1)
        pairs = (blocks - begin + 1) // 2

        def pair(i, carry):
            b = begin + 2 * i
            at = p * blocks + b
            second = b + 1 < blocks
            pos = b * block_len - window
            emit(
                n + 1 + i,
                p,
                at,
                jnp.where(second, at + 1, at),
                pos,
                jnp.where(second, pos + block_len, FAR),
                0,
            )
            return carry

        lax.fori_loop(0, pairs, pair, 0)
        plan_ref[LAST, p] = n + pairs
        return n + 1 + pairs

    n = lax.fori_loop(0, prompts, prompt, 0)

    def pad(i, carry):
        emit(i, 0, 0, 0, FAR, FAR, 1)
        return carry

    lax.fori_loop(n, steps, pad, 0)
    for c in fills:
        c.wait()


def main_kernel(
    sizes,
    order_ref,
    plan_ref,
    len_ref,
    slot_ref,
    gain_ref,
    tok_hbm,
    wq_hbm,
    wkv_hbm,
    wout_hbm,
    cache_hbm,
    mixed_ref,
    land_ref,
    slot_out,
    tok,
    wq,
    wkv,
    kvb,
    *scratch,
):
    layers = land_ref.shape[0]
    caches = (kvb,) + scratch[: layers - 1]
    run(
        sizes,
        (order_ref, plan_ref, len_ref, slot_ref, gain_ref),
        (tok_hbm, wq_hbm, wkv_hbm, wout_hbm, cache_hbm),
        (mixed_ref, land_ref, slot_out),
        (tok, wq, wkv, kvb, caches),
        *scratch[layers - 1 :],
    )


def run(
    sizes,
    scalars,
    args,
    outs,
    bufs,
    pack,
    wall,
    q_ref,
    acc_ref,
    max_ref,
    sum_ref,
    stat_ref,
    attn,
    attn_in,
    total_ref,
    load_sem,
    own_sem,
    z1_send,
    z1_recv,
    z2_send,
    z2_recv,
    xy_send,
    xy_recv,
    s1_send,
    s1_recv,
    s2_send,
    s2_recv,
    hand_send,
    hand_recv,
    slot_send,
    slot_recv,
    at_send,
    at_recv,
):
    order_ref, plan_ref, len_ref, slot_ref, gain_ref = scalars
    tok_hbm, wq_hbm, wkv_hbm, wout_hbm, cache_hbm = args
    mixed_ref, land_ref, slot_out = outs
    tok, wq, wkv, kvb, caches = bufs
    G, DP, T = sizes
    R = G * DP
    g, d, t = lax.axis_index("group"), lax.axis_index("dp"), lax.axis_index("tensor")
    r = g * DP + d
    core = d % CORES
    sib = d + 1 - 2 * core
    layers = land_ref.shape[0]
    cap = land_ref.shape[1] // R
    per_dev = cache_hbm.shape[1]
    prompts, rows, width = tok.shape
    groups, _, qrows, lanes = q_ref.shape
    heads = qrows // rows
    steps = plan_ref.shape[1]
    half = wall.shape[1] // CORES
    rest = half - R1_ROWS
    quarter = width // G

    def load(i, src, dst):
        return pltpu.make_async_copy(src, dst, load_sem.at[i])

    loads = (
        [load(0, cache_hbm.at[0], kvb.at[pl.ds(0, per_dev)])]
        + [load(l, cache_hbm.at[l], caches[l]) for l in range(1, layers)]
        + [
            load(layers, tok_hbm, tok),
            load(layers + 1, wkv_hbm, wkv),
            load(layers + 2, wq_hbm, wq),
            load(layers + 3, wout_hbm, wall.at[t]),
        ]
    )
    for c in loads:
        c.start()

    def remote(src, dst, send, recv, dev):
        return pltpu.make_async_remote_copy(
            src_ref=src, dst_ref=dst, send_sem=send, recv_sem=recv, device_id=dev, device_id_type=MESH
        )

    barrier = pltpu.get_barrier_semaphore()

    def hello(e, carry):
        to = r ^ e
        pl.semaphore_signal(barrier, 1, device_id=(to // DP, to % DP, t), device_id_type=MESH)
        return carry

    lax.fori_loop(1, R, hello, 0)
    for k in range(1, T):
        pl.semaphore_signal(barrier, 1, device_id=(g, d, (t + k) % T), device_id_type=MESH)
    pl.semaphore_wait(barrier, R - 1 + T - 1)

    mine1 = pl.ds(pl.multiple_of(core * half, 16), R1_ROWS)
    mine2 = pl.ds(pl.multiple_of(core * half + R1_ROWS, 16), rest)
    cols2 = pl.ds(pl.multiple_of(g * quarter, 128), quarter)

    def origin(k):
        return (t + T - k) % T

    def z1(up):
        to, k = (t + 1, 1) if up else (t - 1, T - 1)
        return remote(
            wout_hbm.at[mine1],
            wall.at[t, mine1],
            z1_send.at[T - 1 + up],
            z1_recv.at[k - 1],
            (g, d, to),
        )

    def forward(k):
        o = origin(k)
        to = jnp.where(o < t, t + 1, t - 1)
        part = wall.at[o, mine1]
        return remote(part, part, z1_send.at[k - 1], z1_recv.at[(to - o + T) % T - 1], (g, d, to))

    def passes_on(k):
        o = origin(k)
        return ((o < t) & (t < T - 1)) | ((o > t) & (t > 0))

    def line(distance):
        for k in range(1, T):

            @pl.when(abs(origin(k) - t) == distance)
            def _():
                part = wall.at[origin(k), mine1]
                remote(part, part, z1_send.at[k - 1], z1_recv.at[k - 1], (g, d, t ^ 1)).wait_recv()

                @pl.when(passes_on(k))
                def _():
                    forward(k).start()

                s1(k).start()

    def z2(k):
        return remote(
            wout_hbm.at[mine2, cols2],
            wall.at[t, mine2, cols2],
            z2_send.at[k - 1],
            z2_recv.at[k - 1],
            (g, d, (t + k) % T),
        )

    def xy(k, e):
        part = wall.at[origin(k), mine2, cols2]
        i = (k - 1) * (G - 1) + e - 1
        return remote(part, part, xy_send.at[i], xy_recv.at[i], (g ^ e, d, t))

    def s1(k):
        part = wall.at[origin(k), mine1]
        return remote(part, part, s1_send.at[k - 1], s1_recv.at[k - 1], (g, sib, t))

    def s2(k):
        part = wall.at[origin(k), mine2]
        return remote(part, part, s2_send.at[k - 1], s2_recv.at[k - 1], (g, sib, t))

    def hand(l, e):
        to = r ^ e
        return remote(
            pack.at[l, pl.ds(to * cap, cap)],
            land_ref.at[l, pl.ds(r * cap, cap)],
            hand_send.at[l, e],
            hand_recv.at[l, e],
            (to // DP, to % DP, t),
        )

    def slots(e):
        to = r ^ e
        return remote(
            slot_ref.at[to], slot_out.at[r], slot_send.at[e], slot_recv.at[e], (to // DP, to % DP, t)
        )

    def exchange(n, k):
        i = n * (T - 1) + k - 1
        pairs = heads // 2
        to = (t + k) % T
        return remote(
            attn.at[to, pl.ds(n * pairs, pairs)],
            attn_in.at[t, pl.ds(n * pairs, pairs)],
            at_send.at[i],
            at_recv.at[i],
            (g, d, to),
        )

    pl.when(t < T - 1)(lambda: z1(True).start())
    pl.when(t > 0)(lambda: z1(False).start())

    def hello_slots(e, carry):
        slots(e).start()
        return carry

    lax.fori_loop(1, R, hello_slots, 0)
    own_slots = pltpu.make_async_copy(slot_ref.at[r], slot_out.at[r], own_sem.at[layers])
    own_slots.start()

    def own(l):
        span = pl.ds(r * cap, cap)
        return pltpu.make_async_copy(pack.at[l, span], land_ref.at[l, span], own_sem.at[l])

    for l in range(layers):
        loads[l].wait()

        def put(i, carry):
            pack[l, i] = caches[l][order_ref[i]]
            return carry

        lax.fori_loop(0, R * cap, put, 0)

        def send(e, carry):
            hand(l, e).start()
            return carry

        lax.fori_loop(1, R, send, 0)
        own(l).start()

    for k in range(1, T):
        z2(k).start()

    loads[layers].wait()
    loads[layers + 1].wait()
    loads[layers + 2].wait()
    low = lax.broadcasted_iota(jnp.int32, (rows, lanes), 1) < HD

    gains = gain_ref[...].astype(jnp.float32)
    gain = jnp.concatenate([gains[i : i + 1] for i in range(gains.shape[0])], axis=1)

    def project(p, carry):
        x = tok[p].astype(jnp.float32)
        inv = lax.rsqrt(jnp.mean(x * x, axis=-1, keepdims=True) + EPS)
        normed = (x * inv * gain).astype(jnp.bfloat16)
        kv = jnp.dot(normed, wkv[...], preferred_element_type=jnp.float32).astype(jnp.bfloat16)
        kvb[pl.ds(per_dev + 2 * p, 2)] = kv.reshape(2, rows // 2, lanes)
        q = jnp.dot(normed, wq[...], preferred_element_type=jnp.float32) * (1.0 / HD**0.5)
        for pair in range(q.shape[1] // lanes):
            both = q[:, pair * lanes : (pair + 1) * lanes]
            n, at = (2 * pair) // heads, (2 * pair) % heads
            q_ref[n, p, at * rows : (at + 1) * rows] = jnp.where(low, both, 0.0).astype(jnp.bfloat16)
            q_ref[n, p, (at + 1) * rows : (at + 2) * rows] = jnp.where(
                low, pltpu.roll(both, HD, 1), 0.0
            ).astype(jnp.bfloat16)
        return carry

    lax.fori_loop(0, prompts, project, 0)

    trans = (((1,), (1,)), ((), ()))
    block_len = kvb.shape[1]
    keys = 2 * block_len
    window = per_dev // prompts * block_len
    acc_ref[0] = jnp.zeros(acc_ref.shape[1:], acc_ref.dtype)
    max_ref[0] = jnp.full(max_ref.shape[1:], NEG, max_ref.dtype)
    sum_ref[0] = jnp.zeros(sum_ref.shape[1:], sum_ref.dtype)

    def pair(i):
        return jnp.concatenate([kvb[plan_ref[KEY0, i]], kvb[plan_ref[KEY1, i]]], axis=0)

    def place(i, key):
        return jnp.where(key < block_len, plan_ref[POS0, i] + key, plan_ref[POS1, i] + (key - block_len))

    def seen(i, at, query):
        oldest = -len_ref[0, plan_ref[PROMPT, i]]
        return (at <= query) & (at >= jnp.maximum(query + (1 - window), oldest))

    down = lax.broadcasted_iota(jnp.int32, (keys, 1), 0)
    across = lax.broadcasted_iota(jnp.int32, (1, keys), 1)
    query_down = lax.broadcasted_iota(jnp.int32, (rows, 1), 0)
    query_across = lax.broadcasted_iota(jnp.int32, (1, rows), 1)

    def measure(n, begin, end):
        def step(i, carry):
            p = plan_ref[PROMPT, i]
            kv = pair(i)
            visible = seen(i, place(i, down), query_across)
            first = plan_ref[FIRST, i] == 1
            for h in range(heads):
                q = q_ref[n, p, h * rows : (h + 1) * rows]
                s = lax.dot_general(kv, q, trans, preferred_element_type=jnp.float32)
                s = jnp.where(visible, s, NEG).reshape(keys // 8, 8, rows)
                before = jnp.where(first, NEG, max_ref[i, h])
                m = jnp.maximum(before, jnp.max(s, axis=0))
                total = jnp.sum(jnp.exp(s - m[None]), axis=0)
                sum_ref[i + 1, h] = sum_ref[i, h] * jnp.exp(before - m) + total
                max_ref[i + 1, h] = m
            return carry

        lax.fori_loop(begin, end, step, 0)

    def stand(x):
        return jnp.broadcast_to(x, (lanes, rows)).T

    def settle():
        def one(p, carry):
            end = plan_ref[LAST, p] + 1
            for h in range(heads):
                m8 = max_ref[end, h]
                m = jnp.max(m8, axis=0, keepdims=True)
                total = jnp.sum(sum_ref[end, h] * jnp.exp(m8 - m), axis=0, keepdims=True)
                stat_ref[0, p, h] = stand(m)
                stat_ref[1, p, h] = stand(1.0 / total)
            return carry

        lax.fori_loop(0, prompts, one, 0)

    def weigh(n, begin, end):
        def step(i, carry):
            p = plan_ref[PROMPT, i]
            kv = pair(i)
            visible = seen(i, place(i, across), query_down)
            keep = jnp.where(plan_ref[FIRST, i] == 1, 0.0, 1.0)
            for h in range(heads):
                q = q_ref[n, p, h * rows : (h + 1) * rows]
                s = lax.dot_general(q, kv, trans, preferred_element_type=jnp.float32)
                s = jnp.where(visible, s, NEG)
                m, inv = stat_ref[0, p, h], stat_ref[1, p, h]
                e = jnp.exp(s - jnp.concatenate([m, m], axis=1))
                w = (e * jnp.concatenate([inv, inv], axis=1)).astype(jnp.bfloat16)
                o = jnp.dot(w, kv, preferred_element_type=jnp.float32)
                acc_ref[i + 1, h] = acc_ref[i, h] * keep + o
            return carry

        lax.fori_loop(begin, end, step, 0)

    def finish(n):
        def one(p, carry):
            live = lax.broadcasted_iota(jnp.int32, (rows, lanes), 0) < len_ref[1, p]
            end = plan_ref[LAST, p] + 1
            for i in range(heads // 2):
                even, odd = acc_ref[end, 2 * i], acc_ref[end, 2 * i + 1]
                both = jnp.where(live, jnp.where(low, pltpu.roll(even, HD, 1), odd), 0.0)
                attn[p, n * (heads // 2) + i] = both.astype(jnp.bfloat16)
            return carry

        lax.fori_loop(0, prompts, one, 0)
        for k in range(1, T):
            exchange(n, k).start()

    def plane():
        for k in range(1, T):
            z2(k).wait_recv()
            for e in range(1, G):
                xy(k, e).start()

    def nothing():
        return None

    turns = (
        (nothing, lambda: line(1), plane, nothing),
        (nothing, lambda: line(2), nothing, nothing),
    )
    middle = steps // 2
    for n in range(groups):
        turn = turns[n] if n < len(turns) else (nothing,) * 4
        measure(n, 0, middle)
        turn[0]()
        measure(n, middle, steps)
        settle()
        turn[1]()
        weigh(n, 0, middle)
        turn[2]()
        weigh(n, middle, steps)
        finish(n)
        turn[3]()

    for k in range(1, T):
        for e in range(1, G):
            xy(k, e).wait_recv()
        s2(k).start()

    def mix(part, o, begin):
        a = jnp.concatenate([part[i] for i in range(part.shape[0])], axis=1)

        def tile(j, carry):
            at = pl.ds(pl.multiple_of(j * total_ref.shape[2], 128), total_ref.shape[2])
            term = jnp.dot(a, wall[o, :, at], preferred_element_type=jnp.float32)
            total_ref[j] = term if begin else total_ref[j] + term
            return carry

        lax.fori_loop(0, total_ref.shape[0], tile, 0)

    loads[layers + 3].wait()
    mix(attn.at[t], t, True)
    line(T - 1)
    for k in range(1, T):
        s1(k).wait_recv()
        s2(k).wait_recv()
        for n in range(groups):
            exchange(n, k).wait_recv()
        mix(attn_in.at[origin(k)], origin(k), False)
    for j in range(total_ref.shape[0]):
        w = total_ref.shape[2]
        mixed_ref[:, j * w : (j + 1) * w] = total_ref[j].astype(jnp.bfloat16)

    for k in range(1, T):
        z2(k).wait_send()
        pl.when(passes_on(k))(lambda k=k: forward(k).wait_send())
        s1(k).wait_send()
        s2(k).wait_send()
        for e in range(1, G):
            xy(k, e).wait_send()
        for n in range(groups):
            exchange(n, k).wait_send()
    pl.when(t < T - 1)(lambda: z1(True).wait_send())
    pl.when(t > 0)(lambda: z1(False).wait_send())
    own_slots.wait()

    def done(e, carry):
        slots(e).wait()
        for l in range(layers):
            hand(l, e).wait()
        return carry

    lax.fori_loop(1, R, done, 0)
    for l in range(layers):
        own(l).wait()


R1_ROWS = 128


def place_kernel(slot_ref, land_ref, mixed_ref, blank_ref, out_ref, done_ref, sems, last_sem):
    total = land_ref.shape[1]
    cap = total // slot_ref.shape[0]
    last = pltpu.make_async_copy(mixed_ref, done_ref, last_sem)

    def one(j):
        slot = slot_ref[j // cap, j % cap, 0]
        return pltpu.make_async_copy(land_ref.at[:, j], out_ref.at[:, slot], sems.at[j])

    def send(j, carry):
        one(j).start()
        return carry

    lax.fori_loop(0, total, send, 0)
    last.start()

    def done(j, carry):
        one(j).wait()
        return carry

    lax.fori_loop(0, total, done, 0)
    last.wait()


def per_device(tokens, norm_gain, w_query, w_keyval, w_out, kv_cache, lengths, dest_slot):
    prompts = lengths.shape[0]
    all_rows, width = tokens.shape
    rows = all_rows // prompts
    layers, _, blocks_win, block_len, lanes = kv_cache.shape
    per_dev = prompts * blocks_win
    G, DP, T = lax.axis_size("group"), lax.axis_size("dp"), lax.axis_size("tensor")
    R = G * DP
    cap = per_dev // R // 2
    live = R * cap
    steps = prompts + (live + prompts) // 2
    heads = w_query.shape[1] // HD
    groups = heads // GROUP_HEADS
    bf, f32 = jnp.bfloat16, jnp.float32

    smem = pl.BlockSpec(memory_space=pltpu.SMEM)
    hbm = pl.BlockSpec(memory_space=pltpu.HBM)
    vmem = pl.BlockSpec(memory_space=pltpu.VMEM)
    dest_t, len_t = dest_slot.T, lengths.T
    order, plan, slots, blank = pl.pallas_call(
        plan_kernel,
        in_specs=[smem, smem],
        out_specs=[smem, smem, vmem, hbm],
        out_shape=[
            jax.ShapeDtypeStruct((live,), jnp.int32),
            jax.ShapeDtypeStruct((7, steps), jnp.int32),
            jax.ShapeDtypeStruct((R, 8, 128), jnp.int32),
            jax.ShapeDtypeStruct((layers, per_dev, block_len, lanes), bf),
        ],
        scratch_shapes=[
            pltpu.SMEM((R,), jnp.int32),
            pltpu.VMEM((per_dev // 2, block_len, lanes), bf),
            pltpu.SemaphoreType.DMA((layers, 2)),
        ],
        name="plan",
    )(dest_t, len_t)

    sem = pltpu.SemaphoreType.DMA
    depth = w_out.shape[0]
    mixed, landed, slots_in = pl.pallas_call(
        functools.partial(main_kernel, (G, DP, T)),
        in_specs=[smem, smem, smem, vmem, vmem] + [hbm] * 5,
        out_specs=[vmem, vmem, vmem],
        out_shape=[
            jax.ShapeDtypeStruct((rows, width), bf),
            jax.ShapeDtypeStruct((layers, live, block_len, lanes), bf),
            jax.ShapeDtypeStruct((R, 8, 128), jnp.int32),
        ],
        scratch_shapes=[
            pltpu.VMEM((prompts, rows, width), bf),
            pltpu.VMEM(w_query.shape, bf),
            pltpu.VMEM(w_keyval.shape, bf),
            pltpu.VMEM((per_dev + 2 * prompts, block_len, lanes), bf),
            *[pltpu.VMEM((per_dev, block_len, lanes), bf) for _ in range(layers - 1)],
            pltpu.VMEM((layers, live, block_len, lanes), bf),
            pltpu.VMEM((T, depth, width), bf),
            pltpu.VMEM((groups, prompts, GROUP_HEADS * rows, lanes), bf),
            pltpu.VMEM((steps + 1, GROUP_HEADS, rows, lanes), f32),
            pltpu.VMEM((steps + 1, GROUP_HEADS, 8, rows), f32),
            pltpu.VMEM((steps + 1, GROUP_HEADS, 8, rows), f32),
            pltpu.VMEM((2, prompts, GROUP_HEADS, rows, lanes), f32),
            pltpu.VMEM((prompts, heads // 2, rows, lanes), bf),
            pltpu.VMEM((T, heads // 2, rows, lanes), bf),
            pltpu.VMEM((4, rows, width // 4), f32),
            sem((layers + 4,)),
            sem((layers + 1,)),
            sem((T + 1,)),
            sem((T - 1,)),
            sem((T - 1,)),
            sem((T - 1,)),
            sem(((T - 1) * (G - 1),)),
            sem(((T - 1) * (G - 1),)),
            sem((T - 1,)),
            sem((T - 1,)),
            sem((T - 1,)),
            sem((T - 1,)),
            sem((layers, R)),
            sem((layers, R)),
            sem((R,)),
            sem((R,)),
            sem((groups * (T - 1),)),
            sem((groups * (T - 1),)),
        ],
        compiler_params=pltpu.CompilerParams(
            collective_id=0, has_side_effects=True, vmem_limit_bytes=VMEM_LIMIT
        ),
        name="main",
    )(
        order,
        plan,
        len_t,
        slots,
        norm_gain.reshape(-1, lanes),
        tokens.reshape(prompts, rows, width),
        w_query,
        w_keyval,
        w_out,
        kv_cache.reshape(layers, per_dev, block_len, lanes),
    )

    decode_cache, mixed = pl.pallas_call(
        place_kernel,
        in_specs=[smem, vmem, vmem, hbm],
        out_specs=[hbm, hbm],
        out_shape=[
            jax.ShapeDtypeStruct((layers, per_dev, block_len, lanes), bf),
            jax.ShapeDtypeStruct((rows, width), bf),
        ],
        scratch_shapes=[sem((live,)), sem],
        input_output_aliases={3: 0},
        compiler_params=pltpu.CompilerParams(vmem_limit_bytes=VMEM_LIMIT),
        name="place",
    )(slots_in, landed, mixed, blank)
    return (mixed, decode_cache)


def solution(mesh):
    in_specs = (
        P(("group", "dp"), None),
        P(),
        P(None, "tensor"),
        P(None, "tensor"),
        P("tensor", None),
        P(None, ("group", "dp"), None, None, "tensor"),
        P(("group", "dp"), None),
        P(),
    )
    out_specs = (P(("group", "dp", "tensor"), None), P(None, ("group", "dp"), None, "tensor"))
    return jax.shard_map(
        per_device, mesh=mesh, in_specs=in_specs, out_specs=out_specs, check_vma=False
    )
```

```python
import functools

import jax
import jax.numpy as jnp
from jax import lax
from jax.experimental import pallas as pl
from jax.experimental.pallas import tpu as pltpu
from jax.sharding import PartitionSpec as P

HD = 64
EPS = 1e-05
NEG = -1e30
FAR = -(1 << 20)
VMEM_LIMIT = 60 * 1024 * 1024
MESH = pl.DeviceIdType.MESH
GROUP_HEADS = 4
CORES = 2

PROMPT, KEY0, KEY1, POS0, POS1, FIRST, LAST = range(7)


def turn_of(j, t, T):
    low = t < T // 2
    if j < T // 2:
        return jnp.where(low, T - 1 - j, j)
    if j < T - 1:
        return jnp.where(low, T // 2 - 1 - t, 3 * (T // 2) - 1 - t)
    return t


def plan_kernel(dest_ref, len_ref, order_ref, plan_ref, slot_ref, count_ref):
    blocks, all_prompts = dest_ref.shape
    prompts = len_ref.shape[1]
    per_dev = prompts * blocks
    devices = slot_ref.shape[0]
    cap = order_ref.shape[0] // devices
    steps = plan_ref.shape[1]
    me = lax.axis_index("group") * lax.axis_size("dp") + lax.axis_index("dp")
    block_len = 128
    window = blocks * block_len

    def clear(i, carry):
        count_ref[i] = 0
        return carry

    lax.fori_loop(0, devices, clear, 0)

    def first_block(p):
        return (window - len_ref[0, p]) // block_len

    def emit(n, p, k0, k1, at0, at1, new):
        plan_ref[PROMPT, n] = p
        plan_ref[KEY0, n] = k0
        plan_ref[KEY1, n] = k1
        plan_ref[POS0, n] = at0
        plan_ref[POS1, n] = at1
        plan_ref[FIRST, n] = new

    def prompt(p, n):
        begin = first_block(p)

        def block(b, carry):
            dest = dest_ref[b, me * prompts + p]
            peer = dest // per_dev
            k = peer * cap + count_ref[peer]
            count_ref[peer] = count_ref[peer] + 1
            order_ref[k] = p * blocks + b
            slot_ref[peer, pl.ds(k - peer * cap, 1), :] = jnp.full(
                (1, 128), dest - peer * per_dev, jnp.int32
            )
            return carry

        lax.fori_loop(begin, blocks, block, 0)
        fresh = per_dev + 2 * p
        emit(n, p, fresh, fresh + 1, 0, block_len, 1)
        pairs = (blocks - begin + 1) // 2

        def pair(i, carry):
            b = begin + 2 * i
            at = p * blocks + b
            second = b + 1 < blocks
            pos = b * block_len - window
            emit(
                n + 1 + i,
                p,
                at,
                jnp.where(second, at + 1, at),
                pos,
                jnp.where(second, pos + block_len, FAR),
                0,
            )
            return carry

        lax.fori_loop(0, pairs, pair, 0)
        plan_ref[LAST, p] = n + pairs
        return n + 1 + pairs

    t, T = lax.axis_index("tensor"), lax.axis_size("tensor")
    n = 0
    for j in range(prompts):
        n = prompt(turn_of(j, t, T), n)

    def pad(i, carry):
        emit(i, 0, 0, 0, FAR, FAR, 1)
        return carry

    lax.fori_loop(n, steps, pad, 0)


def main_kernel(
    sizes,
    order_ref,
    plan_ref,
    len_ref,
    slot_ref,
    gain_ref,
    tok_hbm,
    wq_hbm,
    wkv_hbm,
    wout_hbm,
    cache_hbm,
    mixed_ref,
    land_ref,
    slot_out,
    tok,
    wq,
    wkv,
    kvb,
    *scratch,
):
    layers = land_ref.shape[0]
    caches = (kvb,) + scratch[: layers - 1]
    run(
        sizes,
        (order_ref, plan_ref, len_ref, slot_ref, gain_ref),
        (tok_hbm, wq_hbm, wkv_hbm, wout_hbm, cache_hbm),
        (mixed_ref, land_ref, slot_out),
        (tok, wq, wkv, kvb, caches),
        *scratch[layers - 1 :],
    )


def run(
    sizes,
    scalars,
    args,
    outs,
    bufs,
    pack,
    wall,
    q_ref,
    acc_ref,
    max_ref,
    sum_ref,
    stat_ref,
    attn,
    attn_in,
    total_ref,
    load_sem,
    own_sem,
    z1_send,
    z1_recv,
    z2_send,
    z2_recv,
    xy_send,
    xy_recv,
    s1_send,
    s1_recv,
    s2_send,
    s2_recv,
    hand_send,
    hand_recv,
    slot_send,
    slot_recv,
    at_send,
    at_recv,
):
    order_ref, plan_ref, len_ref, slot_ref, gain_ref = scalars
    tok_hbm, wq_hbm, wkv_hbm, wout_hbm, cache_hbm = args
    mixed_ref, land_ref, slot_out = outs
    tok, wq, wkv, kvb, caches = bufs
    G, DP, T = sizes
    R = G * DP
    g, d, t = lax.axis_index("group"), lax.axis_index("dp"), lax.axis_index("tensor")
    r = g * DP + d
    core = d % CORES
    sib = d + 1 - 2 * core
    layers = land_ref.shape[0]
    cap = land_ref.shape[1] // R
    per_dev = cache_hbm.shape[1]
    prompts, rows, width = tok.shape
    groups, _, qrows, lanes = q_ref.shape
    heads = qrows // rows
    steps = plan_ref.shape[1]
    half = wall.shape[1] // CORES
    rest = half - R1_ROWS
    quarter = width // G

    def load(i, src, dst):
        return pltpu.make_async_copy(src, dst, load_sem.at[i])

    takes = [load(l, cache_hbm.at[l], caches[l].at[pl.ds(0, per_dev)]) for l in range(layers)]
    weights = [load(layers, wkv_hbm, wkv), load(layers + 1, wq_hbm, wq)]
    own_shard = load(layers + 2, wout_hbm, wall.at[t])

    def take_tokens(p):
        return pltpu.make_async_copy(tok_hbm.at[p], tok.at[p], load_sem.at[layers + 3 + p])

    takes[0].start()
    take_tokens(0).start()
    for c in weights:
        c.start()
    for p in range(1, prompts):
        take_tokens(p).start()
    for c in takes[1:]:
        c.start()
    own_shard.start()

    def remote(src, dst, send, recv, dev):
        return pltpu.make_async_remote_copy(
            src_ref=src, dst_ref=dst, send_sem=send, recv_sem=recv, device_id=dev, device_id_type=MESH
        )

    barrier = pltpu.get_barrier_semaphore()

    def hello(e, carry):
        to = r ^ e
        pl.semaphore_signal(barrier, 1, device_id=(to // DP, to % DP, t), device_id_type=MESH)
        return carry

    lax.fori_loop(1, R, hello, 0)
    for k in range(1, T):
        pl.semaphore_signal(barrier, 1, device_id=(g, d, (t + k) % T), device_id_type=MESH)
    pl.semaphore_wait(barrier, R - 1 + T - 1)

    mine1 = pl.ds(pl.multiple_of(core * half, 16), R1_ROWS)
    mine2 = pl.ds(pl.multiple_of(core * half + R1_ROWS, 16), rest)
    cols2 = pl.ds(pl.multiple_of(g * quarter, 128), quarter)

    def origin(k):
        return (t + T - k) % T

    def z1(up):
        to, k = (t + 1, 1) if up else (t - 1, T - 1)
        return remote(
            wout_hbm.at[mine1],
            wall.at[t, mine1],
            z1_send.at[T - 1 + up],
            z1_recv.at[k - 1],
            (g, d, to),
        )

    def forward(k):
        o = origin(k)
        to = jnp.where(o < t, t + 1, t - 1)
        part = wall.at[o, mine1]
        return remote(part, part, z1_send.at[k - 1], z1_recv.at[(to - o + T) % T - 1], (g, d, to))

    def passes_on(k):
        o = origin(k)
        return ((o < t) & (t < T - 1)) | ((o > t) & (t > 0))

    def line(distance):
        for k in range(1, T):

            @pl.when(abs(origin(k) - t) == distance)
            def _():
                part = wall.at[origin(k), mine1]
                remote(part, part, z1_send.at[k - 1], z1_recv.at[k - 1], (g, d, t ^ 1)).wait_recv()

                @pl.when(passes_on(k))
                def _():
                    forward(k).start()

                s1(k).start()

    def z2(k):
        return remote(
            wout_hbm.at[mine2, cols2],
            wall.at[t, mine2, cols2],
            z2_send.at[k - 1],
            z2_recv.at[k - 1],
            (g, d, (t + k) % T),
        )

    def xy(k, e):
        part = wall.at[origin(k), mine2, cols2]
        i = (k - 1) * (G - 1) + e - 1
        return remote(part, part, xy_send.at[i], xy_recv.at[i], (g ^ e, d, t))

    def s1(k):
        part = wall.at[origin(k), mine1]
        return remote(part, part, s1_send.at[k - 1], s1_recv.at[k - 1], (g, sib, t))

    def s2(k):
        part = wall.at[origin(k), mine2]
        return remote(part, part, s2_send.at[k - 1], s2_recv.at[k - 1], (g, sib, t))

    def hand(l, e):
        to = r ^ e
        return remote(
            pack.at[l, pl.ds(to * cap, cap)],
            land_ref.at[l, pl.ds(r * cap, cap)],
            hand_send.at[l, e],
            hand_recv.at[l, e],
            (to // DP, to % DP, t),
        )

    def slots(e):
        to = r ^ e
        return remote(
            slot_ref.at[to], slot_out.at[r], slot_send.at[e], slot_recv.at[e], (to // DP, to % DP, t)
        )

    def exchange(n, to):
        pairs = heads // 2
        k = (to - t + T) % T
        i = n * (T - 1) + k - 1
        return remote(
            attn.at[to, pl.ds(n * pairs, pairs)],
            attn_in.at[t, pl.ds(n * pairs, pairs)],
            at_send.at[i],
            at_recv.at[i],
            (g, d, to),
        )

    pl.when(t < T - 1)(lambda: z1(True).start())
    pl.when(t > 0)(lambda: z1(False).start())

    def hello_slots(e, carry):
        slots(e).start()
        return carry

    lax.fori_loop(1, R, hello_slots, 0)
    own_slots = pltpu.make_async_copy(slot_ref.at[r], slot_out.at[r], own_sem.at[layers])
    own_slots.start()

    def own(l):
        span = pl.ds(r * cap, cap)
        return pltpu.make_async_copy(pack.at[l, span], land_ref.at[l, span], own_sem.at[l])

    def hand_over(l):
        takes[l].wait()

        def put(i, carry):
            pack[l, i] = caches[l][order_ref[i]]
            return carry

        lax.fori_loop(0, R * cap, put, 0)

        def send(e, carry):
            hand(l, e).start()
            return carry

        lax.fori_loop(1, R, send, 0)
        own(l).start()

    hand_over(0)

    for c in weights:
        c.wait()
    low = lax.broadcasted_iota(jnp.int32, (rows, lanes), 1) < HD

    gains = gain_ref[...].astype(jnp.float32)
    gain = jnp.concatenate([gains[i : i + 1] for i in range(gains.shape[0])], axis=1)

    def project(p, carry):
        take_tokens(p).wait()
        x = tok[p].astype(jnp.float32)
        inv = lax.rsqrt(jnp.mean(x * x, axis=-1, keepdims=True) + EPS)
        normed = (x * inv * gain).astype(jnp.bfloat16)
        kv = jnp.dot(normed, wkv[...], preferred_element_type=jnp.float32).astype(jnp.bfloat16)
        kvb[pl.ds(per_dev + 2 * p, 2)] = kv.reshape(2, rows // 2, lanes)
        q = jnp.dot(normed, wq[...], preferred_element_type=jnp.float32) * (1.0 / HD**0.5)
        for pair in range(q.shape[1] // lanes):
            both = q[:, pair * lanes : (pair + 1) * lanes]
            n, at = (2 * pair) // heads, (2 * pair) % heads
            q_ref[n, p, at * rows : (at + 1) * rows] = jnp.where(low, both, 0.0).astype(jnp.bfloat16)
            q_ref[n, p, (at + 1) * rows : (at + 2) * rows] = jnp.where(
                low, pltpu.roll(both, HD, 1), 0.0
            ).astype(jnp.bfloat16)
        return carry

    lax.fori_loop(0, prompts, project, 0)
    for k in range(1, T):
        z2(k).start()
    for l in range(1, layers):
        hand_over(l)

    trans = (((1,), (1,)), ((), ()))
    block_len = kvb.shape[1]
    keys = 2 * block_len
    window = per_dev // prompts * block_len
    acc_ref[0] = jnp.zeros(acc_ref.shape[1:], acc_ref.dtype)
    max_ref[0] = jnp.full(max_ref.shape[1:], NEG, max_ref.dtype)
    sum_ref[0] = jnp.zeros(sum_ref.shape[1:], sum_ref.dtype)

    def pair(i):
        return jnp.concatenate([kvb[plan_ref[KEY0, i]], kvb[plan_ref[KEY1, i]]], axis=0)

    def place(i, key):
        return jnp.where(key < block_len, plan_ref[POS0, i] + key, plan_ref[POS1, i] + (key - block_len))

    def seen(i, at, query):
        oldest = -len_ref[0, plan_ref[PROMPT, i]]
        return (at <= query) & (at >= jnp.maximum(query + (1 - window), oldest))

    down = lax.broadcasted_iota(jnp.int32, (keys, 1), 0)
    across = lax.broadcasted_iota(jnp.int32, (1, keys), 1)
    query_down = lax.broadcasted_iota(jnp.int32, (rows, 1), 0)
    query_across = lax.broadcasted_iota(jnp.int32, (1, rows), 1)

    def measure(n, begin, end):
        def step(i, carry):
            p = plan_ref[PROMPT, i]
            kv = pair(i)
            visible = seen(i, place(i, down), query_across)
            first = plan_ref[FIRST, i] == 1
            for h in range(heads):
                q = q_ref[n, p, h * rows : (h + 1) * rows]
                s = lax.dot_general(kv, q, trans, preferred_element_type=jnp.float32)
                s = jnp.where(visible, s, NEG).reshape(keys // 8, 8, rows)
                before = jnp.where(first, NEG, max_ref[i, h])
                m = jnp.maximum(before, jnp.max(s, axis=0))
                total = jnp.sum(jnp.exp(s - m[None]), axis=0)
                sum_ref[i + 1, h] = sum_ref[i, h] * jnp.exp(before - m) + total
                max_ref[i + 1, h] = m
            return carry

        def two(j, carry):
            step(begin + 2 * j, carry)
            return step(begin + 2 * j + 1, carry)

        lax.fori_loop(0, (end - begin) // 2, two, 0)

    def stand(x):
        return jnp.broadcast_to(x, (lanes, rows)).T

    def settle():
        def one(p, carry):
            end = plan_ref[LAST, p] + 1
            for h in range(heads):
                m8 = max_ref[end, h]
                m = jnp.max(m8, axis=0, keepdims=True)
                total = jnp.sum(sum_ref[end, h] * jnp.exp(m8 - m), axis=0, keepdims=True)
                stat_ref[0, p, h] = stand(m)
                stat_ref[1, p, h] = stand(1.0 / total)
            return carry

        lax.fori_loop(0, prompts, one, 0)

    def weigh(n, begin, end):
        def step(i, carry):
            p = plan_ref[PROMPT, i]
            kv = pair(i)
            visible = seen(i, place(i, across), query_down)
            keep = jnp.where(plan_ref[FIRST, i] == 1, 0.0, 1.0)
            for h in range(heads):
                q = q_ref[n, p, h * rows : (h + 1) * rows]
                s = lax.dot_general(q, kv, trans, preferred_element_type=jnp.float32)
                s = jnp.where(visible, s, NEG)
                m, inv = stat_ref[0, p, h], stat_ref[1, p, h]
                e = jnp.exp(s - jnp.concatenate([m, m], axis=1))
                w = (e * jnp.concatenate([inv, inv], axis=1)).astype(jnp.bfloat16)
                o = jnp.dot(w, kv, preferred_element_type=jnp.float32)
                acc_ref[i + 1, h] = acc_ref[i, h] * keep + o
            return carry

        def two(j, carry):
            step(begin + 2 * j, carry)
            return step(begin + 2 * j + 1, carry)

        lax.fori_loop(0, (end - begin) // 2, two, 0)

    def finish(n, j):
        p = turn_of(j, t, T)
        live = lax.broadcasted_iota(jnp.int32, (rows, lanes), 0) < len_ref[1, p]
        end = plan_ref[LAST, p] + 1
        for i in range(heads // 2):
            even, odd = acc_ref[end, 2 * i], acc_ref[end, 2 * i + 1]
            both = jnp.where(live, jnp.where(low, pltpu.roll(even, HD, 1), odd), 0.0)
            attn[p, n * (heads // 2) + i] = both.astype(jnp.bfloat16)
        if j < prompts - 1:
            exchange(n, p).start()

    def plane():
        for k in range(1, T):
            z2(k).wait_recv()
            for e in range(1, G):
                xy(k, e).start()

    def nothing():
        return None

    turns = (
        (nothing, lambda: line(1), plane, nothing),
        (nothing, lambda: line(2), nothing, nothing),
    )
    longest = window // keys + 1
    middle = steps // 4 * 2
    marks = [min(-(-longest * (j + 1) // 2) * 2, steps) for j in range(2)]
    for n in range(groups):
        turn = turns[n] if n < len(turns) else (nothing,) * 4
        measure(n, 0, middle)
        turn[0]()
        measure(n, middle, steps)
        settle()
        turn[1]()
        weigh(n, 0, marks[0])
        finish(n, 0)
        turn[2]()
        weigh(n, marks[0], marks[1])
        finish(n, 1)
        turn[3]()
        weigh(n, marks[1], steps)
        for j in range(2, prompts):
            finish(n, j)

    for k in range(1, T):
        for e in range(1, G):
            xy(k, e).wait_recv()
        s2(k).start()

    def mix(part, o, begin, last):
        a = jnp.concatenate([part[i] for i in range(part.shape[0])], axis=1)
        w = total_ref.shape[2]

        def tile(j, carry):
            at = pl.ds(pl.multiple_of(j * w, 128), w)
            term = jnp.dot(a, wall[o, :, at], preferred_element_type=jnp.float32)
            total = term if begin else total_ref[j] + term
            if last:
                mixed_ref[:, at] = total.astype(jnp.bfloat16)
            else:
                total_ref[j] = total
            return carry

        lax.fori_loop(0, total_ref.shape[0], tile, 0)

    own_shard.wait()
    mix(attn.at[t], t, True, False)
    line(T - 1)
    for k in range(1, T):
        s1(k).wait_recv()
        s2(k).wait_recv()
        for n in range(groups):
            i = n * (T - 1) + k - 1
            part = attn_in.at[origin(k), pl.ds(n * (heads // 2), heads // 2)]
            remote(part, part, at_send.at[i], at_recv.at[i], (g, d, origin(k))).wait_recv()
        mix(attn_in.at[origin(k)], origin(k), False, k == T - 1)

    for k in range(1, T):
        z2(k).wait_send()
        pl.when(passes_on(k))(lambda k=k: forward(k).wait_send())
        s1(k).wait_send()
        s2(k).wait_send()
        for e in range(1, G):
            xy(k, e).wait_send()
        for n in range(groups):
            exchange(n, (t + k) % T).wait_send()
    pl.when(t < T - 1)(lambda: z1(True).wait_send())
    pl.when(t > 0)(lambda: z1(False).wait_send())
    own_slots.wait()

    def done(e, carry):
        slots(e).wait()
        for l in range(layers):
            hand(l, e).wait()
        return carry

    lax.fori_loop(1, R, done, 0)
    for l in range(layers):
        own(l).wait()


R1_ROWS = 128


def place_kernel(
    slot_ref, land_ref, mixed_ref, out_ref, done_ref, src_ref, zero_ref, held_ref, loads, out_sem, last_sem
):
    layers, slots, block_len, _ = out_ref.shape
    total = land_ref.shape[1]
    sources = slot_ref.shape[0]
    cap = total // sources
    last = pltpu.make_async_copy(mixed_ref, done_ref, last_sem)

    def load(s):
        span = pl.ds(s * cap, cap)
        return pltpu.make_async_copy(land_ref.at[:, span], held_ref.at[:, span], loads.at[s])

    def begin(s, carry):
        load(s).start()
        return carry

    lax.fori_loop(0, sources, begin, 0)
    zero_ref[...] = jnp.zeros_like(zero_ref)

    def clear(j, carry):
        src_ref[j] = -1
        return carry

    lax.fori_loop(0, slots, clear, 0)

    def note(j, carry):
        src_ref[slot_ref[j // cap, j % cap, 0]] = j
        return carry

    lax.fori_loop(0, total, note, 0)

    def fill(j, carry):
        @pl.when(src_ref[j] < 0)
        def _():
            pltpu.make_async_copy(zero_ref, out_ref.at[:, j], out_sem).start()

        return carry

    lax.fori_loop(0, slots, fill, 0)
    last.start()

    def send(s, carry):
        load(s).wait()
        for k in range(cap):
            slot = slot_ref[s, k, 0]
            pltpu.make_async_copy(
                held_ref.at[:, s * cap + k], out_ref.at[:, slot], out_sem
            ).start()
        return carry

    lax.fori_loop(0, sources, send, 0)

    pltpu.make_async_copy(out_ref, out_ref, out_sem).wait()
    last.wait()


def per_device(tokens, norm_gain, w_query, w_keyval, w_out, kv_cache, lengths, dest_slot):
    prompts = lengths.shape[0]
    all_rows, width = tokens.shape
    rows = all_rows // prompts
    layers, _, blocks_win, block_len, lanes = kv_cache.shape
    per_dev = prompts * blocks_win
    G, DP, T = lax.axis_size("group"), lax.axis_size("dp"), lax.axis_size("tensor")
    R = G * DP
    cap = per_dev // R // 2
    live = R * cap
    steps = -(-(prompts + (live + prompts) // 2) // 2) * 2
    heads = w_query.shape[1] // HD
    groups = heads // GROUP_HEADS
    bf, f32 = jnp.bfloat16, jnp.float32

    smem = pl.BlockSpec(memory_space=pltpu.SMEM)
    hbm = pl.BlockSpec(memory_space=pltpu.HBM)
    vmem = pl.BlockSpec(memory_space=pltpu.VMEM)
    dest_t, len_t = dest_slot.T, lengths.T
    order, plan, slots = pl.pallas_call(
        plan_kernel,
        in_specs=[smem, smem],
        out_specs=[smem, smem, vmem],
        out_shape=[
            jax.ShapeDtypeStruct((live,), jnp.int32),
            jax.ShapeDtypeStruct((7, steps), jnp.int32),
            jax.ShapeDtypeStruct((R, 8, 128), jnp.int32),
        ],
        scratch_shapes=[pltpu.SMEM((R,), jnp.int32)],
        name="plan",
    )(dest_t, len_t)

    sem = pltpu.SemaphoreType.DMA
    depth = w_out.shape[0]
    mixed, landed, slots_in = pl.pallas_call(
        functools.partial(main_kernel, (G, DP, T)),
        in_specs=[smem, smem, smem, vmem, vmem] + [hbm] * 5,
        out_specs=[vmem, hbm, vmem],
        out_shape=[
            jax.ShapeDtypeStruct((rows, width), bf),
            jax.ShapeDtypeStruct((layers, live, block_len, lanes), bf),
            jax.ShapeDtypeStruct((R, 8, 128), jnp.int32),
        ],
        scratch_shapes=[
            pltpu.VMEM((prompts, rows, width), bf),
            pltpu.VMEM(w_query.shape, bf),
            pltpu.VMEM(w_keyval.shape, bf),
            pltpu.VMEM((per_dev + 2 * prompts, block_len, lanes), bf),
            *[pltpu.VMEM((per_dev, block_len, lanes), bf) for _ in range(layers - 1)],
            pltpu.VMEM((layers, live, block_len, lanes), bf),
            pltpu.VMEM((T, depth, width), bf),
            pltpu.VMEM((groups, prompts, GROUP_HEADS * rows, lanes), bf),
            pltpu.VMEM((steps + 1, GROUP_HEADS, rows, lanes), f32),
            pltpu.VMEM((steps + 1, GROUP_HEADS, 8, rows), f32),
            pltpu.VMEM((steps + 1, GROUP_HEADS, 8, rows), f32),
            pltpu.VMEM((2, prompts, GROUP_HEADS, rows, lanes), f32),
            pltpu.VMEM((prompts, heads // 2, rows, lanes), bf),
            pltpu.VMEM((T, heads // 2, rows, lanes), bf),
            pltpu.VMEM((4, rows, width // 4), f32),
            sem((layers + 3 + prompts,)),
            sem((layers + 1,)),
            sem((T + 1,)),
            sem((T - 1,)),
            sem((T - 1,)),
            sem((T - 1,)),
            sem(((T - 1) * (G - 1),)),
            sem(((T - 1) * (G - 1),)),
            sem((T - 1,)),
            sem((T - 1,)),
            sem((T - 1,)),
            sem((T - 1,)),
            sem((layers, R)),
            sem((layers, R)),
            sem((R,)),
            sem((R,)),
            sem((groups * (T - 1),)),
            sem((groups * (T - 1),)),
        ],
        compiler_params=pltpu.CompilerParams(
            collective_id=0, has_side_effects=True, vmem_limit_bytes=VMEM_LIMIT
        ),
        name="main",
    )(
        order,
        plan,
        len_t,
        slots,
        norm_gain.reshape(-1, lanes),
        tokens.reshape(prompts, rows, width),
        w_query,
        w_keyval,
        w_out,
        kv_cache.reshape(layers, per_dev, block_len, lanes),
    )

    decode_cache, mixed = pl.pallas_call(
        place_kernel,
        in_specs=[smem, hbm, vmem],
        out_specs=[hbm, hbm],
        out_shape=[
            jax.ShapeDtypeStruct((layers, per_dev, block_len, lanes), bf),
            jax.ShapeDtypeStruct((rows, width), bf),
        ],
        scratch_shapes=[
            pltpu.SMEM((per_dev,), jnp.int32),
            pltpu.VMEM((layers, block_len, lanes), bf),
            pltpu.VMEM((layers, live, block_len, lanes), bf),
            sem((R,)),
            sem,
            sem,
        ],
        compiler_params=pltpu.CompilerParams(vmem_limit_bytes=VMEM_LIMIT),
        name="place",
    )(slots_in, landed, mixed)
    return (mixed, decode_cache)


def solution(mesh):
    in_specs = (
        P(("group", "dp"), None),
        P(),
        P(None, "tensor"),
        P(None, "tensor"),
        P("tensor", None),
        P(None, ("group", "dp"), None, None, "tensor"),
        P(("group", "dp"), None),
        P(),
    )
    out_specs = (P(("group", "dp", "tensor"), None), P(None, ("group", "dp"), None, "tensor"))
    return jax.shard_map(
        per_device, mesh=mesh, in_specs=in_specs, out_specs=out_specs, check_vma=False
    )
```

```python
import functools

import jax
import jax.numpy as jnp
from jax import lax
from jax.experimental import pallas as pl
from jax.experimental.pallas import tpu as pltpu
from jax.sharding import PartitionSpec as P

HD = 64
EPS = 1e-05
NEG = -1e30
FAR = -(1 << 20)
VMEM_LIMIT = 60 * 1024 * 1024
MESH = pl.DeviceIdType.MESH
GROUP_HEADS = 4
CORES = 2

PROMPT, KEY0, KEY1, POS0, POS1, FIRST, LAST = range(7)


def turn_of(j, t, T):
    low = t < T // 2
    if j < T // 2:
        return jnp.where(low, T - 1 - j, j)
    if j < T - 1:
        return jnp.where(low, T // 2 - 1 - t, 3 * (T // 2) - 1 - t)
    return t


def plan_kernel(dest_ref, len_ref, order_ref, plan_ref, slot_ref, count_ref):
    blocks, all_prompts = dest_ref.shape
    prompts = len_ref.shape[1]
    per_dev = prompts * blocks
    devices = slot_ref.shape[0]
    cap = order_ref.shape[0] // devices
    steps = plan_ref.shape[1]
    me = lax.axis_index("group") * lax.axis_size("dp") + lax.axis_index("dp")
    block_len = 128
    window = blocks * block_len

    def clear(i, carry):
        count_ref[i] = 0
        return carry

    lax.fori_loop(0, devices, clear, 0)

    def first_block(p):
        return (window - len_ref[0, p]) // block_len

    def emit(n, p, k0, k1, at0, at1, new):
        plan_ref[PROMPT, n] = p
        plan_ref[KEY0, n] = k0
        plan_ref[KEY1, n] = k1
        plan_ref[POS0, n] = at0
        plan_ref[POS1, n] = at1
        plan_ref[FIRST, n] = new

    def prompt(p, n):
        begin = first_block(p)

        def block(b, carry):
            dest = dest_ref[b, me * prompts + p]
            peer = dest // per_dev
            k = peer * cap + count_ref[peer]
            count_ref[peer] = count_ref[peer] + 1
            order_ref[k] = p * blocks + b
            slot_ref[peer, pl.ds(k - peer * cap, 1), :] = jnp.full(
                (1, 128), dest - peer * per_dev, jnp.int32
            )
            return carry

        lax.fori_loop(begin, blocks, block, 0)
        fresh = per_dev + 2 * p
        emit(n, p, fresh, fresh + 1, 0, block_len, 1)
        pairs = (blocks - begin + 1) // 2

        def pair(i, carry):
            b = begin + 2 * i
            at = p * blocks + b
            second = b + 1 < blocks
            pos = b * block_len - window
            emit(
                n + 1 + i,
                p,
                at,
                jnp.where(second, at + 1, at),
                pos,
                jnp.where(second, pos + block_len, FAR),
                0,
            )
            return carry

        lax.fori_loop(0, pairs, pair, 0)
        plan_ref[LAST, p] = n + pairs
        return n + 1 + pairs

    t, T = lax.axis_index("tensor"), lax.axis_size("tensor")
    n = 0
    for j in range(prompts):
        n = prompt(turn_of(j, t, T), n)

    def pad(i, carry):
        emit(i, 0, 0, 0, FAR, FAR, 1)
        return carry

    lax.fori_loop(n, steps, pad, 0)


def main_kernel(
    sizes,
    order_ref,
    plan_ref,
    len_ref,
    slot_ref,
    gain_ref,
    tok_hbm,
    wq_hbm,
    wkv_hbm,
    wout_hbm,
    cache_hbm,
    mixed_ref,
    land_ref,
    slot_out,
    tok,
    wq,
    wkv,
    kvb,
    *scratch,
):
    layers = land_ref.shape[0]
    caches = (kvb,) + scratch[: layers - 1]
    run(
        sizes,
        (order_ref, plan_ref, len_ref, slot_ref, gain_ref),
        (tok_hbm, wq_hbm, wkv_hbm, wout_hbm, cache_hbm),
        (mixed_ref, land_ref, slot_out),
        (tok, wq, wkv, kvb, caches),
        *scratch[layers - 1 :],
    )


def run(
    sizes,
    scalars,
    args,
    outs,
    bufs,
    pack,
    wall,
    q_ref,
    acc_ref,
    max_ref,
    sum_ref,
    stat_ref,
    attn,
    attn_in,
    total_ref,
    load_sem,
    own_sem,
    z1_send,
    z1_recv,
    z2_send,
    z2_recv,
    xy_send,
    xy_recv,
    across_send,
    across_recv,
    s1_send,
    s1_recv,
    s2_send,
    s2_recv,
    hand_send,
    hand_recv,
    slot_send,
    slot_recv,
    at_send,
    at_recv,
):
    order_ref, plan_ref, len_ref, slot_ref, gain_ref = scalars
    tok_hbm, wq_hbm, wkv_hbm, wout_hbm, cache_hbm = args
    mixed_ref, land_ref, slot_out = outs
    tok, wq, wkv, kvb, caches = bufs
    G, DP, T = sizes
    R = G * DP
    g, d, t = lax.axis_index("group"), lax.axis_index("dp"), lax.axis_index("tensor")
    r = g * DP + d
    core = d % CORES
    sib = d + 1 - 2 * core
    layers = land_ref.shape[0]
    cap = land_ref.shape[1] // R
    per_dev = cache_hbm.shape[1]
    prompts, rows, width = tok.shape
    groups, _, qrows, lanes = q_ref.shape
    heads = qrows // rows
    steps = plan_ref.shape[1]
    half = wall.shape[1] // CORES
    rest = half - R1_ROWS
    quarter = width // G

    def load(i, src, dst):
        return pltpu.make_async_copy(src, dst, load_sem.at[i])

    takes = [load(l, cache_hbm.at[l], caches[l].at[pl.ds(0, per_dev)]) for l in range(layers)]
    weights = [load(layers, wkv_hbm, wkv), load(layers + 1, wq_hbm, wq)]
    own_shard = load(layers + 2, wout_hbm, wall.at[t])

    def take_tokens(p):
        return pltpu.make_async_copy(tok_hbm.at[p], tok.at[p], load_sem.at[layers + 3 + p])

    takes[0].start()
    take_tokens(0).start()
    for c in weights:
        c.start()
    for p in range(1, prompts):
        take_tokens(p).start()
    for c in takes[1:]:
        c.start()
    own_shard.start()

    def remote(src, dst, send, recv, dev):
        return pltpu.make_async_remote_copy(
            src_ref=src, dst_ref=dst, send_sem=send, recv_sem=recv, device_id=dev, device_id_type=MESH
        )

    barrier = pltpu.get_barrier_semaphore()

    def hello(e, carry):
        to = r ^ e
        pl.semaphore_signal(barrier, 1, device_id=(to // DP, to % DP, t), device_id_type=MESH)
        return carry

    lax.fori_loop(1, R, hello, 0)
    for k in range(1, T):
        pl.semaphore_signal(barrier, 1, device_id=(g, d, (t + k) % T), device_id_type=MESH)
    pl.semaphore_wait(barrier, R - 1 + T - 1)

    mine1 = pl.ds(pl.multiple_of(core * half, 16), R1_ROWS)
    mine2 = pl.ds(pl.multiple_of(core * half + R1_ROWS, 16), rest)
    cols2 = pl.ds(pl.multiple_of(g * quarter, 128), quarter)

    def origin(k):
        return (t + T - k) % T

    def z1(up):
        to, k = (t + 1, 1) if up else (t - 1, T - 1)
        return remote(
            wout_hbm.at[mine1],
            wall.at[t, mine1],
            z1_send.at[T - 1 + up],
            z1_recv.at[k - 1],
            (g, d, to),
        )

    def forward(k):
        o = origin(k)
        to = jnp.where(o < t, t + 1, t - 1)
        part = wall.at[o, mine1]
        return remote(part, part, z1_send.at[k - 1], z1_recv.at[(to - o + T) % T - 1], (g, d, to))

    def passes_on(k):
        o = origin(k)
        return ((o < t) & (t < T - 1)) | ((o > t) & (t > 0))

    def line(distance):
        for k in range(1, T):

            @pl.when(abs(origin(k) - t) == distance)
            def _():
                part = wall.at[origin(k), mine1]
                remote(part, part, z1_send.at[k - 1], z1_recv.at[k - 1], (g, d, t ^ 1)).wait_recv()

                @pl.when(passes_on(k))
                def _():
                    forward(k).start()

                s1(k).start()

    def z2(k):
        return remote(
            wout_hbm.at[mine2, cols2],
            wall.at[t, mine2, cols2],
            z2_send.at[k - 1],
            z2_recv.at[k - 1],
            (g, d, (t + k) % T),
        )

    def xy(k, e):
        part = wall.at[origin(k), mine2, cols2]
        i = (k - 1) * 2 + e - 1
        return remote(part, part, xy_send.at[i], xy_recv.at[i], (g ^ e, d, t))

    def pass_on(k, e):
        rows_half = pl.ds(pl.multiple_of(core * half + R1_ROWS + (e - 1) * (rest // 2), 16), rest // 2)
        cols = pl.ds(pl.multiple_of((g ^ e) * quarter, 128), quarter)
        part = wall.at[origin(k), rows_half, cols]
        i = (k - 1) * 2 + e - 1
        return remote(part, part, across_send.at[i], across_recv.at[i], (g ^ (3 - e), d, t))

    def across_in(k, e):
        rows_half = pl.ds(pl.multiple_of(core * half + R1_ROWS + (e - 1) * (rest // 2), 16), rest // 2)
        cols = pl.ds(pl.multiple_of((g ^ 3) * quarter, 128), quarter)
        part = wall.at[origin(k), rows_half, cols]
        i = (k - 1) * 2 + e - 1
        return remote(part, part, across_send.at[i], across_recv.at[i], (g ^ (3 - e), d, t))

    def s1(k):
        part = wall.at[origin(k), mine1]
        return remote(part, part, s1_send.at[k - 1], s1_recv.at[k - 1], (g, sib, t))

    def s2(k):
        part = wall.at[origin(k), mine2]
        return remote(part, part, s2_send.at[k - 1], s2_recv.at[k - 1], (g, sib, t))

    def hand(l, e):
        to = r ^ e
        return remote(
            pack.at[l, pl.ds(to * cap, cap)],
            land_ref.at[l, pl.ds(r * cap, cap)],
            hand_send.at[l, e],
            hand_recv.at[l, e],
            (to // DP, to % DP, t),
        )

    def slots(e):
        to = r ^ e
        return remote(
            slot_ref.at[to], slot_out.at[r], slot_send.at[e], slot_recv.at[e], (to // DP, to % DP, t)
        )

    def exchange(n, to):
        pairs = heads // 2
        k = (to - t + T) % T
        i = n * (T - 1) + k - 1
        return remote(
            attn.at[to, pl.ds(n * pairs, pairs)],
            attn_in.at[t, pl.ds(n * pairs, pairs)],
            at_send.at[i],
            at_recv.at[i],
            (g, d, to),
        )

    for k in range(1, T):
        z2(k).start()

    def hello_slots(e, carry):
        slots(e).start()
        return carry

    lax.fori_loop(1, R, hello_slots, 0)
    own_slots = pltpu.make_async_copy(slot_ref.at[r], slot_out.at[r], own_sem.at[layers])
    own_slots.start()

    def own(l):
        span = pl.ds(r * cap, cap)
        return pltpu.make_async_copy(pack.at[l, span], land_ref.at[l, span], own_sem.at[l])

    def hand_over(l):
        takes[l].wait()

        def put(i, carry):
            pack[l, i] = caches[l][order_ref[i]]
            return carry

        lax.fori_loop(0, R * cap, put, 0)

        def send(e, carry):
            hand(l, e).start()
            return carry

        lax.fori_loop(1, R, send, 0)
        own(l).start()

    hand_over(0)

    for c in weights:
        c.wait()
    low = lax.broadcasted_iota(jnp.int32, (rows, lanes), 1) < HD

    gains = gain_ref[...].astype(jnp.float32)
    gain = jnp.concatenate([gains[i : i + 1] for i in range(gains.shape[0])], axis=1)

    def project(p, carry):
        take_tokens(p).wait()
        x = tok[p].astype(jnp.float32)
        inv = lax.rsqrt(jnp.mean(x * x, axis=-1, keepdims=True) + EPS)
        normed = (x * inv * gain).astype(jnp.bfloat16)
        kv = jnp.dot(normed, wkv[...], preferred_element_type=jnp.float32).astype(jnp.bfloat16)
        kvb[pl.ds(per_dev + 2 * p, 2)] = kv.reshape(2, rows // 2, lanes)
        q = jnp.dot(normed, wq[...], preferred_element_type=jnp.float32) * (1.0 / HD**0.5)
        for pair in range(q.shape[1] // lanes):
            both = q[:, pair * lanes : (pair + 1) * lanes]
            n, at = (2 * pair) // heads, (2 * pair) % heads
            q_ref[n, p, at * rows : (at + 1) * rows] = jnp.where(low, both, 0.0).astype(jnp.bfloat16)
            q_ref[n, p, (at + 1) * rows : (at + 2) * rows] = jnp.where(
                low, pltpu.roll(both, HD, 1), 0.0
            ).astype(jnp.bfloat16)
        return carry

    lax.fori_loop(0, prompts, project, 0)
    pl.when(t < T - 1)(lambda: z1(True).start())
    pl.when(t > 0)(lambda: z1(False).start())
    for l in range(1, layers - 1):
        hand_over(l)

    trans = (((1,), (1,)), ((), ()))
    block_len = kvb.shape[1]
    keys = 2 * block_len
    window = per_dev // prompts * block_len
    acc_ref[0] = jnp.zeros(acc_ref.shape[1:], acc_ref.dtype)
    max_ref[0] = jnp.full(max_ref.shape[1:], NEG, max_ref.dtype)
    sum_ref[0] = jnp.zeros(sum_ref.shape[1:], sum_ref.dtype)

    def pair(i):
        return jnp.concatenate([kvb[plan_ref[KEY0, i]], kvb[plan_ref[KEY1, i]]], axis=0)

    def place(i, key):
        return jnp.where(key < block_len, plan_ref[POS0, i] + key, plan_ref[POS1, i] + (key - block_len))

    def seen(i, at, query):
        oldest = -len_ref[0, plan_ref[PROMPT, i]]
        return (at <= query) & (at >= jnp.maximum(query + (1 - window), oldest))

    down = lax.broadcasted_iota(jnp.int32, (keys, 1), 0)
    across = lax.broadcasted_iota(jnp.int32, (1, keys), 1)
    query_down = lax.broadcasted_iota(jnp.int32, (rows, 1), 0)
    query_across = lax.broadcasted_iota(jnp.int32, (1, rows), 1)

    def measure(n, begin, end):
        def step(i, carry):
            p = plan_ref[PROMPT, i]
            kv = pair(i)
            visible = seen(i, place(i, down), query_across)
            first = plan_ref[FIRST, i] == 1
            for h in range(heads):
                q = q_ref[n, p, h * rows : (h + 1) * rows]
                s = lax.dot_general(kv, q, trans, preferred_element_type=jnp.float32)
                s = jnp.where(visible, s, NEG).reshape(keys // 8, 8, rows)
                before = jnp.where(first, NEG, max_ref[i, h])
                m = jnp.maximum(before, jnp.max(s, axis=0))
                total = jnp.sum(jnp.exp(s - m[None]), axis=0)
                sum_ref[i + 1, h] = sum_ref[i, h] * jnp.exp(before - m) + total
                max_ref[i + 1, h] = m
            return carry

        def two(j, carry):
            step(begin + 2 * j, carry)
            return step(begin + 2 * j + 1, carry)

        lax.fori_loop(0, (end - begin) // 2, two, 0)

    def stand(x):
        return jnp.broadcast_to(x, (lanes, rows)).T

    def settle():
        def one(p, carry):
            end = plan_ref[LAST, p] + 1
            for h in range(heads):
                m8 = max_ref[end, h]
                m = jnp.max(m8, axis=0, keepdims=True)
                total = jnp.sum(sum_ref[end, h] * jnp.exp(m8 - m), axis=0, keepdims=True)
                stat_ref[0, p, h] = stand(m)
                stat_ref[1, p, h] = stand(1.0 / total)
            return carry

        lax.fori_loop(0, prompts, one, 0)

    def weigh(n, begin, end):
        def step(i, carry):
            p = plan_ref[PROMPT, i]
            kv = pair(i)
            visible = seen(i, place(i, across), query_down)
            keep = jnp.where(plan_ref[FIRST, i] == 1, 0.0, 1.0)
            for h in range(heads):
                q = q_ref[n, p, h * rows : (h + 1) * rows]
                s = lax.dot_general(q, kv, trans, preferred_element_type=jnp.float32)
                s = jnp.where(visible, s, NEG)
                m, inv = stat_ref[0, p, h], stat_ref[1, p, h]
                e = jnp.exp(s - jnp.concatenate([m, m], axis=1))
                w = (e * jnp.concatenate([inv, inv], axis=1)).astype(jnp.bfloat16)
                o = jnp.dot(w, kv, preferred_element_type=jnp.float32)
                acc_ref[i + 1, h] = acc_ref[i, h] * keep + o
            return carry

        def two(j, carry):
            step(begin + 2 * j, carry)
            return step(begin + 2 * j + 1, carry)

        lax.fori_loop(0, (end - begin) // 2, two, 0)

    def finish(n, j):
        p = turn_of(j, t, T)
        live = lax.broadcasted_iota(jnp.int32, (rows, lanes), 0) < len_ref[1, p]
        end = plan_ref[LAST, p] + 1
        for i in range(heads // 2):
            even, odd = acc_ref[end, 2 * i], acc_ref[end, 2 * i + 1]
            both = jnp.where(live, jnp.where(low, pltpu.roll(even, HD, 1), odd), 0.0)
            attn[p, n * (heads // 2) + i] = both.astype(jnp.bfloat16)
        if j < prompts - 1:
            exchange(n, p).start()

    def plane():
        for k in range(1, T):
            z2(k).wait_recv()
            for e in (1, 2):
                xy(k, e).start()
        hand_over(layers - 1)

    def corner():
        for k in range(1, T):
            for e in (1, 2):
                xy(k, e).wait_recv()
                pass_on(k, e).start()

    def nothing():
        return None

    turns = (
        (nothing, plane, lambda: line(1), nothing),
        (lambda: line(2), corner, nothing, nothing),
    )
    longest = window // keys + 1
    middle = steps // 4 * 2
    marks = [min(-(-longest * (j + 1) // 2) * 2, steps) for j in range(2)]
    for n in range(groups):
        turn = turns[n] if n < len(turns) else (nothing,) * 4
        measure(n, 0, middle)
        turn[0]()
        measure(n, middle, steps)
        settle()
        turn[1]()
        weigh(n, 0, marks[0])
        finish(n, 0)
        turn[2]()
        weigh(n, marks[0], marks[1])
        finish(n, 1)
        turn[3]()
        weigh(n, marks[1], steps)
        for j in range(2, prompts):
            finish(n, j)

    for k in range(1, T):
        for e in (1, 2):
            across_in(k, e).wait_recv()
        s2(k).start()

    def mix(part, o, begin, last):
        a = jnp.concatenate([part[i] for i in range(part.shape[0])], axis=1)
        w = total_ref.shape[2]

        def tile(j, carry):
            at = pl.ds(pl.multiple_of(j * w, 128), w)
            term = jnp.dot(a, wall[o, :, at], preferred_element_type=jnp.float32)
            total = term if begin else total_ref[j] + term
            if last:
                mixed_ref[:, at] = total.astype(jnp.bfloat16)
            else:
                total_ref[j] = total
            return carry

        lax.fori_loop(0, total_ref.shape[0], tile, 0)

    own_shard.wait()
    mix(attn.at[t], t, True, False)
    outer = (t == 0) | (t == T - 1)
    order = (
        jnp.where(t < T // 2, T - 1, 1),
        jnp.where(outer, 2, jnp.where(t == 1, 1, T - 1)),
        jnp.where(outer, jnp.where(t == 0, 1, T - 1), 2),
    )
    for j, k in enumerate(order):
        if j == T - 2:
            line(T - 1)
        s1(k).wait_recv()
        s2(k).wait_recv()
        for n in range(groups):
            i = n * (T - 1) + k - 1
            part = attn_in.at[origin(k), pl.ds(n * (heads // 2), heads // 2)]
            remote(part, part, at_send.at[i], at_recv.at[i], (g, d, origin(k))).wait_recv()
        mix(attn_in.at[origin(k)], origin(k), False, j == T - 2)

    for k in range(1, T):
        z2(k).wait_send()
        pl.when(passes_on(k))(lambda k=k: forward(k).wait_send())
        s1(k).wait_send()
        s2(k).wait_send()
        for e in (1, 2):
            xy(k, e).wait_send()
            pass_on(k, e).wait_send()
        for n in range(groups):
            exchange(n, (t + k) % T).wait_send()
    pl.when(t < T - 1)(lambda: z1(True).wait_send())
    pl.when(t > 0)(lambda: z1(False).wait_send())
    own_slots.wait()

    def done(e, carry):
        slots(e).wait()
        for l in range(layers):
            hand(l, e).wait()
        return carry

    lax.fori_loop(1, R, done, 0)
    for l in range(layers):
        own(l).wait()


R1_ROWS = 96


def place_kernel(
    slot_ref, land_ref, mixed_ref, out_ref, done_ref, src_ref, zero_ref, held_ref, through_ref, loads, out_sem, last_sem
):
    layers, slots, block_len, _ = out_ref.shape
    total = land_ref.shape[1]
    sources = slot_ref.shape[0]
    cap = total // sources
    first = pltpu.make_async_copy(mixed_ref, through_ref, last_sem)
    last = pltpu.make_async_copy(through_ref, done_ref, last_sem)
    first.start()

    def load(s):
        span = pl.ds(s * cap, cap)
        return pltpu.make_async_copy(land_ref.at[:, span], held_ref.at[:, span], loads.at[s])

    def begin(s, carry):
        load(s).start()
        return carry

    lax.fori_loop(0, sources, begin, 0)
    zero_ref[...] = jnp.zeros_like(zero_ref)

    def clear(j, carry):
        src_ref[j] = -1
        return carry

    lax.fori_loop(0, slots, clear, 0)

    def note(j, carry):
        src_ref[slot_ref[j // cap, j % cap, 0]] = j
        return carry

    lax.fori_loop(0, total, note, 0)

    def fill(j, carry):
        @pl.when(src_ref[j] < 0)
        def _():
            pltpu.make_async_copy(zero_ref, out_ref.at[:, j], out_sem).start()

        return carry

    lax.fori_loop(0, slots, fill, 0)
    first.wait()
    last.start()

    def send(s, carry):
        load(s).wait()
        for k in range(cap):
            slot = slot_ref[s, k, 0]
            pltpu.make_async_copy(
                held_ref.at[:, s * cap + k], out_ref.at[:, slot], out_sem
            ).start()
        return carry

    lax.fori_loop(0, sources, send, 0)

    pltpu.make_async_copy(out_ref, out_ref, out_sem).wait()
    last.wait()


def per_device(tokens, norm_gain, w_query, w_keyval, w_out, kv_cache, lengths, dest_slot):
    prompts = lengths.shape[0]
    all_rows, width = tokens.shape
    rows = all_rows // prompts
    layers, _, blocks_win, block_len, lanes = kv_cache.shape
    per_dev = prompts * blocks_win
    G, DP, T = lax.axis_size("group"), lax.axis_size("dp"), lax.axis_size("tensor")
    R = G * DP
    cap = per_dev // R // 2
    live = R * cap
    steps = -(-(prompts + (live + prompts) // 2) // 2) * 2
    heads = w_query.shape[1] // HD
    groups = heads // GROUP_HEADS
    bf, f32 = jnp.bfloat16, jnp.float32

    smem = pl.BlockSpec(memory_space=pltpu.SMEM)
    hbm = pl.BlockSpec(memory_space=pltpu.HBM)
    vmem = pl.BlockSpec(memory_space=pltpu.VMEM)
    dest_t, len_t = dest_slot.T, lengths.T
    order, plan, slots = pl.pallas_call(
        plan_kernel,
        in_specs=[smem, smem],
        out_specs=[smem, smem, vmem],
        out_shape=[
            jax.ShapeDtypeStruct((live,), jnp.int32),
            jax.ShapeDtypeStruct((7, steps), jnp.int32),
            jax.ShapeDtypeStruct((R, 8, 128), jnp.int32),
        ],
        scratch_shapes=[pltpu.SMEM((R,), jnp.int32)],
        name="plan",
    )(dest_t, len_t)

    sem = pltpu.SemaphoreType.DMA
    depth = w_out.shape[0]
    mixed, landed, slots_in = pl.pallas_call(
        functools.partial(main_kernel, (G, DP, T)),
        in_specs=[smem, smem, smem, vmem, vmem] + [hbm] * 5,
        out_specs=[vmem, hbm, vmem],
        out_shape=[
            jax.ShapeDtypeStruct((rows, width), bf),
            jax.ShapeDtypeStruct((layers, live, block_len, lanes), bf),
            jax.ShapeDtypeStruct((R, 8, 128), jnp.int32),
        ],
        scratch_shapes=[
            pltpu.VMEM((prompts, rows, width), bf),
            pltpu.VMEM(w_query.shape, bf),
            pltpu.VMEM(w_keyval.shape, bf),
            pltpu.VMEM((per_dev + 2 * prompts, block_len, lanes), bf),
            *[pltpu.VMEM((per_dev, block_len, lanes), bf) for _ in range(layers - 1)],
            pltpu.VMEM((layers, live, block_len, lanes), bf),
            pltpu.VMEM((T, depth, width), bf),
            pltpu.VMEM((groups, prompts, GROUP_HEADS * rows, lanes), bf),
            pltpu.VMEM((steps + 1, GROUP_HEADS, rows, lanes), f32),
            pltpu.VMEM((steps + 1, GROUP_HEADS, 8, rows), f32),
            pltpu.VMEM((steps + 1, GROUP_HEADS, 8, rows), f32),
            pltpu.VMEM((2, prompts, GROUP_HEADS, rows, lanes), f32),
            pltpu.VMEM((prompts, heads // 2, rows, lanes), bf),
            pltpu.VMEM((T, heads // 2, rows, lanes), bf),
            pltpu.VMEM((4, rows, width // 4), f32),
            sem((layers + 3 + prompts,)),
            sem((layers + 1,)),
            sem((T + 1,)),
            sem((T - 1,)),
            sem((T - 1,)),
            sem((T - 1,)),
            sem(((T - 1) * 2,)),
            sem(((T - 1) * 2,)),
            sem(((T - 1) * 2,)),
            sem(((T - 1) * 2,)),
            sem((T - 1,)),
            sem((T - 1,)),
            sem((T - 1,)),
            sem((T - 1,)),
            sem((layers, R)),
            sem((layers, R)),
            sem((R,)),
            sem((R,)),
            sem((groups * (T - 1),)),
            sem((groups * (T - 1),)),
        ],
        compiler_params=pltpu.CompilerParams(
            collective_id=0, has_side_effects=True, vmem_limit_bytes=VMEM_LIMIT
        ),
        name="main",
    )(
        order,
        plan,
        len_t,
        slots,
        norm_gain.reshape(-1, lanes),
        tokens.reshape(prompts, rows, width),
        w_query,
        w_keyval,
        w_out,
        kv_cache.reshape(layers, per_dev, block_len, lanes),
    )

    decode_cache, mixed = pl.pallas_call(
        place_kernel,
        in_specs=[smem, hbm, hbm],
        out_specs=[hbm, hbm],
        out_shape=[
            jax.ShapeDtypeStruct((layers, per_dev, block_len, lanes), bf),
            jax.ShapeDtypeStruct((rows, width), bf),
        ],
        scratch_shapes=[
            pltpu.SMEM((per_dev,), jnp.int32),
            pltpu.VMEM((layers, block_len, lanes), bf),
            pltpu.VMEM((layers, live, block_len, lanes), bf),
            pltpu.VMEM((rows, width), bf),
            sem((R,)),
            sem,
            sem,
        ],
        compiler_params=pltpu.CompilerParams(vmem_limit_bytes=VMEM_LIMIT),
        name="place",
    )(slots_in, landed, mixed)
    return (mixed, decode_cache)


def solution(mesh):
    in_specs = (
        P(("group", "dp"), None),
        P(),
        P(None, "tensor"),
        P(None, "tensor"),
        P("tensor", None),
        P(None, ("group", "dp"), None, None, "tensor"),
        P(("group", "dp"), None),
        P(),
    )
    out_specs = (P(("group", "dp", "tensor"), None), P(None, ("group", "dp"), None, "tensor"))
    return jax.shard_map(
        per_device, mesh=mesh, in_specs=in_specs, out_specs=out_specs, check_vma=False
    )
```

```python
import functools

import jax
import jax.numpy as jnp
from jax import lax
from jax.experimental import pallas as pl
from jax.experimental.pallas import tpu as pltpu
from jax.sharding import PartitionSpec as P

HD = 64
EPS = 1e-05
NEG = -1e30
FAR = -(1 << 20)
VMEM_LIMIT = 60 * 1024 * 1024
MESH = pl.DeviceIdType.MESH
GROUP_HEADS = 4
CORES = 2

PROMPT, KEY0, KEY1, POS0, POS1, FIRST, LAST = range(7)


def turn_of(j, t, T):
    low = t < T // 2
    if j < T // 2:
        return jnp.where(low, T - 1 - j, j)
    if j < T - 1:
        return jnp.where(low, T // 2 - 1 - t, 3 * (T // 2) - 1 - t)
    return t


def plan_kernel(dest_ref, len_ref, order_ref, plan_ref, slot_ref, count_ref):
    blocks, all_prompts = dest_ref.shape
    prompts = len_ref.shape[1]
    per_dev = prompts * blocks
    devices = slot_ref.shape[0]
    cap = order_ref.shape[0] // devices
    steps = plan_ref.shape[1]
    me = lax.axis_index("group") * lax.axis_size("dp") + lax.axis_index("dp")
    block_len = 128
    window = blocks * block_len

    def clear(i, carry):
        count_ref[i] = 0
        return carry

    lax.fori_loop(0, devices, clear, 0)

    def first_block(p):
        return (window - len_ref[0, p]) // block_len

    def emit(n, p, k0, k1, at0, at1, new):
        plan_ref[PROMPT, n] = p
        plan_ref[KEY0, n] = k0
        plan_ref[KEY1, n] = k1
        plan_ref[POS0, n] = at0
        plan_ref[POS1, n] = at1
        plan_ref[FIRST, n] = new

    def prompt(p, n):
        begin = first_block(p)

        def block(b, carry):
            dest = dest_ref[b, me * prompts + p]
            peer = dest // per_dev
            k = peer * cap + count_ref[peer]
            count_ref[peer] = count_ref[peer] + 1
            order_ref[k] = p * blocks + b
            slot_ref[peer, pl.ds(k - peer * cap, 1), :] = jnp.full(
                (1, 128), dest - peer * per_dev, jnp.int32
            )
            return carry

        lax.fori_loop(begin, blocks, block, 0)
        fresh = per_dev + 2 * p
        emit(n, p, fresh, fresh + 1, 0, block_len, 1)
        pairs = (blocks - begin + 1) // 2

        def pair(i, carry):
            b = begin + 2 * i
            at = p * blocks + b
            second = b + 1 < blocks
            pos = b * block_len - window
            emit(
                n + 1 + i,
                p,
                at,
                jnp.where(second, at + 1, at),
                pos,
                jnp.where(second, pos + block_len, FAR),
                0,
            )
            return carry

        lax.fori_loop(0, pairs, pair, 0)
        plan_ref[LAST, p] = n + pairs
        return n + 1 + pairs

    t, T = lax.axis_index("tensor"), lax.axis_size("tensor")
    n = 0
    for j in range(prompts):
        n = prompt(turn_of(j, t, T), n)

    def pad(i, carry):
        emit(i, 0, 0, 0, FAR, FAR, 1)
        return carry

    lax.fori_loop(n, steps, pad, 0)


def main_kernel(
    sizes,
    order_ref,
    plan_ref,
    len_ref,
    slot_ref,
    gain_ref,
    tok_hbm,
    wq_hbm,
    wkv_hbm,
    wout_hbm,
    cache_hbm,
    mixed_ref,
    land_ref,
    slot_out,
    tok,
    wq,
    wkv,
    kvb,
    *scratch,
):
    layers = land_ref.shape[0]
    caches = (kvb,) + scratch[: layers - 1]
    run(
        sizes,
        (order_ref, plan_ref, len_ref, slot_ref, gain_ref),
        (tok_hbm, wq_hbm, wkv_hbm, wout_hbm, cache_hbm),
        (mixed_ref, land_ref, slot_out),
        (tok, wq, wkv, kvb, caches),
        *scratch[layers - 1 :],
    )


def run(
    sizes,
    scalars,
    args,
    outs,
    bufs,
    pack,
    wall,
    q_ref,
    acc_ref,
    max_ref,
    sum_ref,
    stat_ref,
    attn,
    attn_in,
    total_ref,
    load_sem,
    own_sem,
    z1_send,
    z1_recv,
    z2_send,
    z2_recv,
    xy_send,
    xy_recv,
    across_send,
    across_recv,
    s1_send,
    s1_recv,
    s2_send,
    s2_recv,
    hand_send,
    hand_recv,
    slot_send,
    slot_recv,
    at_send,
    at_recv,
):
    order_ref, plan_ref, len_ref, slot_ref, gain_ref = scalars
    tok_hbm, wq_hbm, wkv_hbm, wout_hbm, cache_hbm = args
    mixed_ref, land_ref, slot_out = outs
    tok, wq, wkv, kvb, caches = bufs
    G, DP, T = sizes
    R = G * DP
    g, d, t = lax.axis_index("group"), lax.axis_index("dp"), lax.axis_index("tensor")
    r = g * DP + d
    core = d % CORES
    sib = d + 1 - 2 * core
    layers = land_ref.shape[0]
    cap = land_ref.shape[1] // R
    per_dev = cache_hbm.shape[1]
    prompts, rows, width = tok.shape
    groups, _, qrows, lanes = q_ref.shape
    heads = qrows // rows
    steps = plan_ref.shape[1]
    half = wall.shape[1] // CORES
    rest = half - R1_ROWS
    quarter = width // G

    def load(i, src, dst):
        return pltpu.make_async_copy(src, dst, load_sem.at[i])

    takes = [load(l, cache_hbm.at[l], caches[l].at[pl.ds(0, per_dev)]) for l in range(layers)]
    weights = [load(layers, wkv_hbm, wkv), load(layers + 1, wq_hbm, wq)]
    own_shard = load(layers + 2, wout_hbm, wall.at[t])

    def take_tokens(p):
        return pltpu.make_async_copy(tok_hbm.at[p], tok.at[p], load_sem.at[layers + 3 + p])

    takes[0].start()
    take_tokens(0).start()
    for c in weights:
        c.start()
    for p in range(1, prompts):
        take_tokens(p).start()
    for c in takes[1:]:
        c.start()
    own_shard.start()

    def remote(src, dst, send, recv, dev):
        return pltpu.make_async_remote_copy(
            src_ref=src, dst_ref=dst, send_sem=send, recv_sem=recv, device_id=dev, device_id_type=MESH
        )

    barrier = pltpu.get_barrier_semaphore()

    def hello(e, carry):
        to = r ^ e
        pl.semaphore_signal(barrier, 1, device_id=(to // DP, to % DP, t), device_id_type=MESH)
        return carry

    lax.fori_loop(1, R, hello, 0)
    for k in range(1, T):
        pl.semaphore_signal(barrier, 1, device_id=(g, d, (t + k) % T), device_id_type=MESH)
    pl.semaphore_wait(barrier, R - 1 + T - 1)

    mine1 = pl.ds(pl.multiple_of(core * half, 16), R1_ROWS)
    mine2 = pl.ds(pl.multiple_of(core * half + R1_ROWS, 16), rest)
    cols2 = pl.ds(pl.multiple_of(g * quarter, 128), quarter)

    def origin(k):
        return (t + T - k) % T

    def z1(up):
        to, k = (t + 1, 1) if up else (t - 1, T - 1)
        return remote(
            wout_hbm.at[mine1],
            wall.at[t, mine1],
            z1_send.at[T - 1 + up],
            z1_recv.at[k - 1],
            (g, d, to),
        )

    def forward(k):
        o = origin(k)
        to = jnp.where(o < t, t + 1, t - 1)
        part = wall.at[o, mine1]
        return remote(part, part, z1_send.at[k - 1], z1_recv.at[(to - o + T) % T - 1], (g, d, to))

    def passes_on(k):
        o = origin(k)
        return ((o < t) & (t < T - 1)) | ((o > t) & (t > 0))

    def line(distance):
        for k in range(1, T):

            @pl.when(abs(origin(k) - t) == distance)
            def _():
                part = wall.at[origin(k), mine1]
                remote(part, part, z1_send.at[k - 1], z1_recv.at[k - 1], (g, d, t ^ 1)).wait_recv()

                @pl.when(passes_on(k))
                def _():
                    forward(k).start()

                s1(k).start()

    def z2(k):
        return remote(
            wout_hbm.at[mine2, cols2],
            wall.at[t, mine2, cols2],
            z2_send.at[k - 1],
            z2_recv.at[k - 1],
            (g, d, (t + k) % T),
        )

    def xy(k, e):
        part = wall.at[origin(k), mine2, cols2]
        i = (k - 1) * 2 + e - 1
        return remote(part, part, xy_send.at[i], xy_recv.at[i], (g ^ e, d, t))

    def pass_on(k, e):
        rows_half = pl.ds(pl.multiple_of(core * half + R1_ROWS + (e - 1) * (rest // 2), 16), rest // 2)
        cols = pl.ds(pl.multiple_of((g ^ e) * quarter, 128), quarter)
        part = wall.at[origin(k), rows_half, cols]
        i = (k - 1) * 2 + e - 1
        return remote(part, part, across_send.at[i], across_recv.at[i], (g ^ (3 - e), d, t))

    def across_in(k, e):
        rows_half = pl.ds(pl.multiple_of(core * half + R1_ROWS + (e - 1) * (rest // 2), 16), rest // 2)
        cols = pl.ds(pl.multiple_of((g ^ 3) * quarter, 128), quarter)
        part = wall.at[origin(k), rows_half, cols]
        i = (k - 1) * 2 + e - 1
        return remote(part, part, across_send.at[i], across_recv.at[i], (g ^ (3 - e), d, t))

    def s1(k):
        part = wall.at[origin(k), mine1]
        return remote(part, part, s1_send.at[k - 1], s1_recv.at[k - 1], (g, sib, t))

    def s2(k):
        part = wall.at[origin(k), mine2]
        return remote(part, part, s2_send.at[k - 1], s2_recv.at[k - 1], (g, sib, t))

    def hand(l, e):
        to = r ^ e
        return remote(
            pack.at[l, pl.ds(to * cap, cap)],
            land_ref.at[l, pl.ds(r * cap, cap)],
            hand_send.at[l, e],
            hand_recv.at[l, e],
            (to // DP, to % DP, t),
        )

    def slots(e):
        to = r ^ e
        return remote(
            slot_ref.at[to], slot_out.at[r], slot_send.at[e], slot_recv.at[e], (to // DP, to % DP, t)
        )

    def exchange(n, to):
        pairs = heads // 2
        k = (to - t + T) % T
        i = n * (T - 1) + k - 1
        return remote(
            attn.at[to, pl.ds(n * pairs, pairs)],
            attn_in.at[t, pl.ds(n * pairs, pairs)],
            at_send.at[i],
            at_recv.at[i],
            (g, d, to),
        )

    for k in range(1, T):
        z2(k).start()

    def hello_slots(e, carry):
        slots(e).start()
        return carry

    lax.fori_loop(1, R, hello_slots, 0)
    own_slots = pltpu.make_async_copy(slot_ref.at[r], slot_out.at[r], own_sem.at[layers])
    own_slots.start()

    def own(l):
        span = pl.ds(r * cap, cap)
        return pltpu.make_async_copy(pack.at[l, span], land_ref.at[l, span], own_sem.at[l])

    def hand_over(l):
        takes[l].wait()

        def put(i, carry):
            pack[l, i] = caches[l][order_ref[i]]
            return carry

        lax.fori_loop(0, R * cap, put, 0)

        def send(e, carry):
            hand(l, e).start()
            return carry

        lax.fori_loop(1, R, send, 0)
        own(l).start()

    hand_over(0)

    for c in weights:
        c.wait()
    low = lax.broadcasted_iota(jnp.int32, (rows, lanes), 1) < HD

    gains = gain_ref[...].astype(jnp.float32)
    gain = jnp.concatenate([gains[i : i + 1] for i in range(gains.shape[0])], axis=1)

    def project(p, carry):
        take_tokens(p).wait()
        x = tok[p].astype(jnp.float32)
        inv = lax.rsqrt(jnp.mean(x * x, axis=-1, keepdims=True) + EPS)
        normed = (x * inv * gain).astype(jnp.bfloat16)
        kv = jnp.dot(normed, wkv[...], preferred_element_type=jnp.float32).astype(jnp.bfloat16)
        kvb[pl.ds(per_dev + 2 * p, 2)] = kv.reshape(2, rows // 2, lanes)
        q = jnp.dot(normed, wq[...], preferred_element_type=jnp.float32) * (1.0 / HD**0.5)
        for pair in range(q.shape[1] // lanes):
            both = q[:, pair * lanes : (pair + 1) * lanes]
            n, at = (2 * pair) // heads, (2 * pair) % heads
            q_ref[n, p, at * rows : (at + 1) * rows] = jnp.where(low, both, 0.0).astype(jnp.bfloat16)
            q_ref[n, p, (at + 1) * rows : (at + 2) * rows] = jnp.where(
                low, pltpu.roll(both, HD, 1), 0.0
            ).astype(jnp.bfloat16)
        return carry

    lax.fori_loop(0, prompts, project, 0)
    pl.when(t < T - 1)(lambda: z1(True).start())
    pl.when(t > 0)(lambda: z1(False).start())
    for l in range(1, layers - 2):
        hand_over(l)

    trans = (((1,), (1,)), ((), ()))
    block_len = kvb.shape[1]
    keys = 2 * block_len
    window = per_dev // prompts * block_len
    acc_ref[0] = jnp.zeros(acc_ref.shape[1:], acc_ref.dtype)
    max_ref[0] = jnp.full(max_ref.shape[1:], NEG, max_ref.dtype)
    sum_ref[0] = jnp.zeros(sum_ref.shape[1:], sum_ref.dtype)

    def pair(i):
        return jnp.concatenate([kvb[plan_ref[KEY0, i]], kvb[plan_ref[KEY1, i]]], axis=0)

    def place(i, key):
        return jnp.where(key < block_len, plan_ref[POS0, i] + key, plan_ref[POS1, i] + (key - block_len))

    def seen(i, at, query):
        oldest = -len_ref[0, plan_ref[PROMPT, i]]
        return (at <= query) & (at >= jnp.maximum(query + (1 - window), oldest))

    down = lax.broadcasted_iota(jnp.int32, (keys, 1), 0)
    across = lax.broadcasted_iota(jnp.int32, (1, keys), 1)
    query_down = lax.broadcasted_iota(jnp.int32, (rows, 1), 0)
    query_across = lax.broadcasted_iota(jnp.int32, (1, rows), 1)

    def measure(n, begin, end):
        def step(i, carry):
            p = plan_ref[PROMPT, i]
            kv = pair(i)
            visible = seen(i, place(i, down), query_across)
            first = plan_ref[FIRST, i] == 1
            for h in range(heads):
                q = q_ref[n, p, h * rows : (h + 1) * rows]
                s = lax.dot_general(kv, q, trans, preferred_element_type=jnp.float32)
                s = jnp.where(visible, s, NEG).reshape(keys // 8, 8, rows)
                before = jnp.where(first, NEG, max_ref[i, h])
                m = jnp.maximum(before, jnp.max(s, axis=0))
                total = jnp.sum(jnp.exp(s - m[None]), axis=0)
                sum_ref[i + 1, h] = sum_ref[i, h] * jnp.exp(before - m) + total
                max_ref[i + 1, h] = m
            return carry

        def two(j, carry):
            step(begin + 2 * j, carry)
            return step(begin + 2 * j + 1, carry)

        lax.fori_loop(0, (end - begin) // 2, two, 0)

    def stand(x):
        return jnp.broadcast_to(x, (lanes, rows)).T

    def settle():
        def one(p, carry):
            end = plan_ref[LAST, p] + 1
            for h in range(heads):
                m8 = max_ref[end, h]
                m = jnp.max(m8, axis=0, keepdims=True)
                total = jnp.sum(sum_ref[end, h] * jnp.exp(m8 - m), axis=0, keepdims=True)
                stat_ref[0, p, h] = stand(m)
                stat_ref[1, p, h] = stand(1.0 / total)
            return carry

        lax.fori_loop(0, prompts, one, 0)

    def weigh(n, begin, end):
        def step(i, carry):
            p = plan_ref[PROMPT, i]
            kv = pair(i)
            visible = seen(i, place(i, across), query_down)
            keep = jnp.where(plan_ref[FIRST, i] == 1, 0.0, 1.0)
            for h in range(heads):
                q = q_ref[n, p, h * rows : (h + 1) * rows]
                s = lax.dot_general(q, kv, trans, preferred_element_type=jnp.float32)
                s = jnp.where(visible, s, NEG)
                m, inv = stat_ref[0, p, h], stat_ref[1, p, h]
                e = jnp.exp(s - jnp.concatenate([m, m], axis=1))
                w = (e * jnp.concatenate([inv, inv], axis=1)).astype(jnp.bfloat16)
                o = jnp.dot(w, kv, preferred_element_type=jnp.float32)
                acc_ref[i + 1, h] = acc_ref[i, h] * keep + o
            return carry

        def two(j, carry):
            step(begin + 2 * j, carry)
            return step(begin + 2 * j + 1, carry)

        lax.fori_loop(0, (end - begin) // 2, two, 0)

    def finish(n, j):
        p = turn_of(j, t, T)
        live = lax.broadcasted_iota(jnp.int32, (rows, lanes), 0) < len_ref[1, p]
        end = plan_ref[LAST, p] + 1
        for i in range(heads // 2):
            even, odd = acc_ref[end, 2 * i], acc_ref[end, 2 * i + 1]
            both = jnp.where(live, jnp.where(low, pltpu.roll(even, HD, 1), odd), 0.0)
            attn[p, n * (heads // 2) + i] = both.astype(jnp.bfloat16)
        if j < prompts - 1:
            exchange(n, p).start()

    def plane():
        for k in range(1, T):
            z2(k).wait_recv()
            for e in (1, 2):
                xy(k, e).start()
        hand_over(layers - 2)

    def corner():
        for k in range(1, T):
            for e in (1, 2):
                xy(k, e).wait_recv()
                pass_on(k, e).start()
        hand_over(layers - 1)

    def nothing():
        return None

    turns = (
        (nothing, plane, lambda: line(1), nothing),
        (lambda: line(2), corner, nothing, nothing),
    )
    longest = window // keys + 1
    middle = steps // 4 * 2
    marks = [min(-(-longest * (j + 1) // 2) * 2, steps) for j in range(2)]
    for n in range(groups):
        turn = turns[n] if n < len(turns) else (nothing,) * 4
        measure(n, 0, middle)
        turn[0]()
        measure(n, middle, steps)
        settle()
        turn[1]()
        weigh(n, 0, marks[0])
        finish(n, 0)
        turn[2]()
        weigh(n, marks[0], marks[1])
        finish(n, 1)
        turn[3]()
        weigh(n, marks[1], steps)
        for j in range(2, prompts):
            finish(n, j)

    for k in range(1, T):
        for e in (1, 2):
            across_in(k, e).wait_recv()
        s2(k).start()

    def mix(part, o, begin, last):
        a = jnp.concatenate([part[i] for i in range(part.shape[0])], axis=1)
        w = total_ref.shape[2]

        def tile(j, carry):
            at = pl.ds(pl.multiple_of(j * w, 128), w)
            term = jnp.dot(a, wall[o, :, at], preferred_element_type=jnp.float32)
            total = term if begin else total_ref[j] + term
            if last:
                mixed_ref[:, at] = total.astype(jnp.bfloat16)
            else:
                total_ref[j] = total
            return carry

        lax.fori_loop(0, total_ref.shape[0], tile, 0)

    own_shard.wait()
    mix(attn.at[t], t, True, False)
    outer = (t == 0) | (t == T - 1)
    order = (
        jnp.where(t < T // 2, T - 1, 1),
        jnp.where(outer, 2, jnp.where(t == 1, 1, T - 1)),
        jnp.where(outer, jnp.where(t == 0, 1, T - 1), 2),
    )
    for j, k in enumerate(order):
        if j == T - 2:
            line(T - 1)
        s1(k).wait_recv()
        s2(k).wait_recv()
        for n in range(groups):
            i = n * (T - 1) + k - 1
            part = attn_in.at[origin(k), pl.ds(n * (heads // 2), heads // 2)]
            remote(part, part, at_send.at[i], at_recv.at[i], (g, d, origin(k))).wait_recv()
        mix(attn_in.at[origin(k)], origin(k), False, j == T - 2)

    for k in range(1, T):
        z2(k).wait_send()
        pl.when(passes_on(k))(lambda k=k: forward(k).wait_send())
        s1(k).wait_send()
        s2(k).wait_send()
        for e in (1, 2):
            xy(k, e).wait_send()
            pass_on(k, e).wait_send()
        for n in range(groups):
            exchange(n, (t + k) % T).wait_send()
    pl.when(t < T - 1)(lambda: z1(True).wait_send())
    pl.when(t > 0)(lambda: z1(False).wait_send())
    own_slots.wait()

    def done(e, carry):
        slots(e).wait()
        for l in range(layers):
            hand(l, e).wait()
        return carry

    lax.fori_loop(1, R, done, 0)
    for l in range(layers):
        own(l).wait()


R1_ROWS = 96


def place_kernel(
    slot_ref, land_ref, mixed_ref, out_ref, done_ref, src_ref, zero_ref, held_ref, through_ref, loads, out_sem, last_sem
):
    layers, slots, block_len, _ = out_ref.shape
    total = land_ref.shape[1]
    sources = slot_ref.shape[0]
    cap = total // sources
    first = pltpu.make_async_copy(mixed_ref, through_ref, last_sem)
    last = pltpu.make_async_copy(through_ref, done_ref, last_sem)
    first.start()

    def load(s):
        span = pl.ds(s * cap, cap)
        return pltpu.make_async_copy(land_ref.at[:, span], held_ref.at[:, span], loads.at[s])

    def begin(s, carry):
        load(s).start()
        return carry

    lax.fori_loop(0, sources, begin, 0)
    zero_ref[...] = jnp.zeros_like(zero_ref)

    def clear(j, carry):
        src_ref[j] = -1
        return carry

    lax.fori_loop(0, slots, clear, 0)

    def note(j, carry):
        src_ref[slot_ref[j // cap, j % cap, 0]] = j
        return carry

    lax.fori_loop(0, total, note, 0)

    def fill(j, carry):
        @pl.when(src_ref[j] < 0)
        def _():
            pltpu.make_async_copy(zero_ref, out_ref.at[:, j], out_sem).start()

        return carry

    lax.fori_loop(0, slots, fill, 0)
    first.wait()
    last.start()

    def send(s, carry):
        load(s).wait()
        for k in range(cap):
            slot = slot_ref[s, k, 0]
            pltpu.make_async_copy(
                held_ref.at[:, s * cap + k], out_ref.at[:, slot], out_sem
            ).start()
        return carry

    lax.fori_loop(0, sources, send, 0)

    pltpu.make_async_copy(out_ref, out_ref, out_sem).wait()
    last.wait()


def per_device(tokens, norm_gain, w_query, w_keyval, w_out, kv_cache, lengths, dest_slot):
    prompts = lengths.shape[0]
    all_rows, width = tokens.shape
    rows = all_rows // prompts
    layers, _, blocks_win, block_len, lanes = kv_cache.shape
    per_dev = prompts * blocks_win
    G, DP, T = lax.axis_size("group"), lax.axis_size("dp"), lax.axis_size("tensor")
    R = G * DP
    cap = per_dev // R // 2
    live = R * cap
    steps = -(-(prompts + (live + prompts) // 2) // 2) * 2
    heads = w_query.shape[1] // HD
    groups = heads // GROUP_HEADS
    bf, f32 = jnp.bfloat16, jnp.float32

    smem = pl.BlockSpec(memory_space=pltpu.SMEM)
    hbm = pl.BlockSpec(memory_space=pltpu.HBM)
    vmem = pl.BlockSpec(memory_space=pltpu.VMEM)
    dest_t, len_t = dest_slot.T, lengths.T
    order, plan, slots = pl.pallas_call(
        plan_kernel,
        in_specs=[smem, smem],
        out_specs=[smem, smem, vmem],
        out_shape=[
            jax.ShapeDtypeStruct((live,), jnp.int32),
            jax.ShapeDtypeStruct((7, steps), jnp.int32),
            jax.ShapeDtypeStruct((R, 8, 128), jnp.int32),
        ],
        scratch_shapes=[pltpu.SMEM((R,), jnp.int32)],
        name="plan",
    )(dest_t, len_t)

    sem = pltpu.SemaphoreType.DMA
    depth = w_out.shape[0]
    mixed, landed, slots_in = pl.pallas_call(
        functools.partial(main_kernel, (G, DP, T)),
        in_specs=[smem, smem, smem, vmem, vmem] + [hbm] * 5,
        out_specs=[vmem, hbm, vmem],
        out_shape=[
            jax.ShapeDtypeStruct((rows, width), bf),
            jax.ShapeDtypeStruct((layers, live, block_len, lanes), bf),
            jax.ShapeDtypeStruct((R, 8, 128), jnp.int32),
        ],
        scratch_shapes=[
            pltpu.VMEM((prompts, rows, width), bf),
            pltpu.VMEM(w_query.shape, bf),
            pltpu.VMEM(w_keyval.shape, bf),
            pltpu.VMEM((per_dev + 2 * prompts, block_len, lanes), bf),
            *[pltpu.VMEM((per_dev, block_len, lanes), bf) for _ in range(layers - 1)],
            pltpu.VMEM((layers, live, block_len, lanes), bf),
            pltpu.VMEM((T, depth, width), bf),
            pltpu.VMEM((groups, prompts, GROUP_HEADS * rows, lanes), bf),
            pltpu.VMEM((steps + 1, GROUP_HEADS, rows, lanes), f32),
            pltpu.VMEM((steps + 1, GROUP_HEADS, 8, rows), f32),
            pltpu.VMEM((steps + 1, GROUP_HEADS, 8, rows), f32),
            pltpu.VMEM((2, prompts, GROUP_HEADS, rows, lanes), f32),
            pltpu.VMEM((prompts, heads // 2, rows, lanes), bf),
            pltpu.VMEM((T, heads // 2, rows, lanes), bf),
            pltpu.VMEM((4, rows, width // 4), f32),
            sem((layers + 3 + prompts,)),
            sem((layers + 1,)),
            sem((T + 1,)),
            sem((T - 1,)),
            sem((T - 1,)),
            sem((T - 1,)),
            sem(((T - 1) * 2,)),
            sem(((T - 1) * 2,)),
            sem(((T - 1) * 2,)),
            sem(((T - 1) * 2,)),
            sem((T - 1,)),
            sem((T - 1,)),
            sem((T - 1,)),
            sem((T - 1,)),
            sem((layers, R)),
            sem((layers, R)),
            sem((R,)),
            sem((R,)),
            sem((groups * (T - 1),)),
            sem((groups * (T - 1),)),
        ],
        compiler_params=pltpu.CompilerParams(
            collective_id=0, has_side_effects=True, vmem_limit_bytes=VMEM_LIMIT
        ),
        name="main",
    )(
        order,
        plan,
        len_t,
        slots,
        norm_gain.reshape(-1, lanes),
        tokens.reshape(prompts, rows, width),
        w_query,
        w_keyval,
        w_out,
        kv_cache.reshape(layers, per_dev, block_len, lanes),
    )

    decode_cache, mixed = pl.pallas_call(
        place_kernel,
        in_specs=[smem, hbm, hbm],
        out_specs=[hbm, hbm],
        out_shape=[
            jax.ShapeDtypeStruct((layers, per_dev, block_len, lanes), bf),
            jax.ShapeDtypeStruct((rows, width), bf),
        ],
        scratch_shapes=[
            pltpu.SMEM((per_dev,), jnp.int32),
            pltpu.VMEM((layers, block_len, lanes), bf),
            pltpu.VMEM((layers, live, block_len, lanes), bf),
            pltpu.VMEM((rows, width), bf),
            sem((R,)),
            sem,
            sem,
        ],
        compiler_params=pltpu.CompilerParams(vmem_limit_bytes=VMEM_LIMIT),
        name="place",
    )(slots_in, landed, mixed)
    return (mixed, decode_cache)


def solution(mesh):
    in_specs = (
        P(("group", "dp"), None),
        P(),
        P(None, "tensor"),
        P(None, "tensor"),
        P("tensor", None),
        P(None, ("group", "dp"), None, None, "tensor"),
        P(("group", "dp"), None),
        P(),
    )
    out_specs = (P(("group", "dp", "tensor"), None), P(None, ("group", "dp"), None, "tensor"))
    return jax.shard_map(
        per_device, mesh=mesh, in_specs=in_specs, out_specs=out_specs, check_vma=False
    )
```

```python
import functools

import jax
import jax.numpy as jnp
from jax import lax
from jax.experimental import pallas as pl
from jax.experimental.pallas import tpu as pltpu
from jax.sharding import PartitionSpec as P

HD = 64
EPS = 1e-05
NEG = -1e30
FAR = -(1 << 20)
VMEM_LIMIT = 60 * 1024 * 1024
MESH = pl.DeviceIdType.MESH
GROUP_HEADS = 4
CORES = 2

PROMPT, KEY0, KEY1, POS0, POS1, FIRST, LAST = range(7)


def turn_of(j, t, T):
    low = t < T // 2
    if j < T // 2:
        return jnp.where(low, T - 1 - j, j)
    if j < T - 1:
        return jnp.where(low, T // 2 - 1 - t, 3 * (T // 2) - 1 - t)
    return t


def plan_kernel(dest_ref, len_ref, order_ref, plan_ref, slot_ref, count_ref):
    blocks, all_prompts = dest_ref.shape
    prompts = len_ref.shape[1]
    per_dev = prompts * blocks
    devices = slot_ref.shape[0]
    cap = order_ref.shape[0] // devices
    steps = plan_ref.shape[1]
    me = lax.axis_index("group") * lax.axis_size("dp") + lax.axis_index("dp")
    block_len = 128
    window = blocks * block_len

    def clear(i, carry):
        count_ref[i] = 0
        return carry

    lax.fori_loop(0, devices, clear, 0)

    def first_block(p):
        return (window - len_ref[0, p]) // block_len

    def emit(n, p, k0, k1, at0, at1, new):
        plan_ref[PROMPT, n] = p
        plan_ref[KEY0, n] = k0
        plan_ref[KEY1, n] = k1
        plan_ref[POS0, n] = at0
        plan_ref[POS1, n] = at1
        plan_ref[FIRST, n] = new

    def prompt(p, n):
        begin = first_block(p)

        def block(b, carry):
            dest = dest_ref[b, me * prompts + p]
            peer = dest // per_dev
            k = peer * cap + count_ref[peer]
            count_ref[peer] = count_ref[peer] + 1
            order_ref[k] = p * blocks + b
            slot_ref[peer, pl.ds(k - peer * cap, 1), :] = jnp.full(
                (1, 128), dest - peer * per_dev, jnp.int32
            )
            return carry

        lax.fori_loop(begin, blocks, block, 0)
        fresh = per_dev + 2 * p
        emit(n, p, fresh, fresh + 1, 0, block_len, 1)
        pairs = (blocks - begin + 1) // 2

        def pair(i, carry):
            b = begin + 2 * i
            at = p * blocks + b
            second = b + 1 < blocks
            pos = b * block_len - window
            emit(
                n + 1 + i,
                p,
                at,
                jnp.where(second, at + 1, at),
                pos,
                jnp.where(second, pos + block_len, FAR),
                0,
            )
            return carry

        lax.fori_loop(0, pairs, pair, 0)
        plan_ref[LAST, p] = n + pairs
        return n + 1 + pairs

    t, T = lax.axis_index("tensor"), lax.axis_size("tensor")
    n = 0
    for j in range(prompts):
        n = prompt(turn_of(j, t, T), n)

    def pad(i, carry):
        emit(i, 0, 0, 0, FAR, FAR, 1)
        return carry

    lax.fori_loop(n, steps, pad, 0)


def main_kernel(
    sizes,
    order_ref,
    plan_ref,
    len_ref,
    slot_ref,
    gain_ref,
    tok_hbm,
    wq_hbm,
    wkv_hbm,
    wout_hbm,
    cache_hbm,
    mixed_ref,
    land_ref,
    slot_out,
    tok,
    wq,
    wkv,
    kvb,
    *scratch,
):
    layers = land_ref.shape[0]
    caches = (kvb,) + scratch[: layers - 1]
    run(
        sizes,
        (order_ref, plan_ref, len_ref, slot_ref, gain_ref),
        (tok_hbm, wq_hbm, wkv_hbm, wout_hbm, cache_hbm),
        (mixed_ref, land_ref, slot_out),
        (tok, wq, wkv, kvb, caches),
        *scratch[layers - 1 :],
    )


def run(
    sizes,
    scalars,
    args,
    outs,
    bufs,
    pack,
    wall,
    q_ref,
    acc_ref,
    max_ref,
    sum_ref,
    stat_ref,
    attn,
    attn_in,
    total_ref,
    load_sem,
    own_sem,
    z1_send,
    z1_recv,
    z2_send,
    z2_recv,
    xy_send,
    xy_recv,
    across_send,
    across_recv,
    s1_send,
    s1_recv,
    s2_send,
    s2_recv,
    hand_send,
    hand_recv,
    slot_send,
    slot_recv,
    at_send,
    at_recv,
):
    order_ref, plan_ref, len_ref, slot_ref, gain_ref = scalars
    tok_hbm, wq_hbm, wkv_hbm, wout_hbm, cache_hbm = args
    mixed_ref, land_ref, slot_out = outs
    tok, wq, wkv, kvb, caches = bufs
    G, DP, T = sizes
    R = G * DP
    g, d, t = lax.axis_index("group"), lax.axis_index("dp"), lax.axis_index("tensor")
    r = g * DP + d
    core = d % CORES
    sib = d + 1 - 2 * core
    layers = land_ref.shape[0]
    cap = land_ref.shape[1] // R
    per_dev = cache_hbm.shape[1]
    prompts, rows, width = tok.shape
    groups, _, qrows, lanes = q_ref.shape
    heads = qrows // rows
    steps = plan_ref.shape[1]
    half = wall.shape[1] // CORES
    rest = half - R1_ROWS
    quarter = width // G

    def load(i, src, dst):
        return pltpu.make_async_copy(src, dst, load_sem.at[i])

    takes = [load(l, cache_hbm.at[l], caches[l].at[pl.ds(0, per_dev)]) for l in range(layers)]
    weights = [load(layers, wkv_hbm, wkv), load(layers + 1, wq_hbm, wq)]
    own_shard = load(layers + 2, wout_hbm, wall.at[t])

    def take_tokens(p):
        return pltpu.make_async_copy(tok_hbm.at[p], tok.at[p], load_sem.at[layers + 3 + p])

    takes[0].start()
    take_tokens(0).start()
    for c in weights:
        c.start()
    for p in range(1, prompts):
        take_tokens(p).start()
    for c in takes[1:]:
        c.start()
    own_shard.start()

    def remote(src, dst, send, recv, dev):
        return pltpu.make_async_remote_copy(
            src_ref=src, dst_ref=dst, send_sem=send, recv_sem=recv, device_id=dev, device_id_type=MESH
        )

    barrier = pltpu.get_barrier_semaphore()

    def hello(e, carry):
        to = r ^ e
        pl.semaphore_signal(barrier, 1, device_id=(to // DP, to % DP, t), device_id_type=MESH)
        return carry

    lax.fori_loop(1, R, hello, 0)
    for k in range(1, T):
        pl.semaphore_signal(barrier, 1, device_id=(g, d, (t + k) % T), device_id_type=MESH)
    pl.semaphore_wait(barrier, R - 1 + T - 1)

    mine1 = pl.ds(pl.multiple_of(core * half, 16), R1_ROWS)
    mine2 = pl.ds(pl.multiple_of(core * half + R1_ROWS, 16), rest)
    cols2 = pl.ds(pl.multiple_of(g * quarter, 128), quarter)

    def origin(k):
        return (t + T - k) % T

    def z1(up):
        to, k = (t + 1, 1) if up else (t - 1, T - 1)
        return remote(
            wout_hbm.at[mine1],
            wall.at[t, mine1],
            z1_send.at[T - 1 + up],
            z1_recv.at[k - 1],
            (g, d, to),
        )

    def forward(k):
        o = origin(k)
        to = jnp.where(o < t, t + 1, t - 1)
        part = wall.at[o, mine1]
        return remote(part, part, z1_send.at[k - 1], z1_recv.at[(to - o + T) % T - 1], (g, d, to))

    def passes_on(k):
        o = origin(k)
        return ((o < t) & (t < T - 1)) | ((o > t) & (t > 0))

    def line(distance):
        for k in range(1, T):

            @pl.when(abs(origin(k) - t) == distance)
            def _():
                part = wall.at[origin(k), mine1]
                remote(part, part, z1_send.at[k - 1], z1_recv.at[k - 1], (g, d, t ^ 1)).wait_recv()

                @pl.when(passes_on(k))
                def _():
                    forward(k).start()

                s1(k).start()

    def z2(k):
        return remote(
            wout_hbm.at[mine2, cols2],
            wall.at[t, mine2, cols2],
            z2_send.at[k - 1],
            z2_recv.at[k - 1],
            (g, d, (t + k) % T),
        )

    def xy(k, e):
        part = wall.at[origin(k), mine2, cols2]
        i = (k - 1) * 2 + e - 1
        return remote(part, part, xy_send.at[i], xy_recv.at[i], (g ^ e, d, t))

    def pass_on(k, e):
        rows_half = pl.ds(pl.multiple_of(core * half + R1_ROWS + (e - 1) * (rest // 2), 16), rest // 2)
        cols = pl.ds(pl.multiple_of((g ^ e) * quarter, 128), quarter)
        part = wall.at[origin(k), rows_half, cols]
        i = (k - 1) * 2 + e - 1
        return remote(part, part, across_send.at[i], across_recv.at[i], (g ^ (3 - e), d, t))

    def across_in(k, e):
        rows_half = pl.ds(pl.multiple_of(core * half + R1_ROWS + (e - 1) * (rest // 2), 16), rest // 2)
        cols = pl.ds(pl.multiple_of((g ^ 3) * quarter, 128), quarter)
        part = wall.at[origin(k), rows_half, cols]
        i = (k - 1) * 2 + e - 1
        return remote(part, part, across_send.at[i], across_recv.at[i], (g ^ (3 - e), d, t))

    def s1(k):
        part = wall.at[origin(k), mine1]
        return remote(part, part, s1_send.at[k - 1], s1_recv.at[k - 1], (g, sib, t))

    def s2(k):
        part = wall.at[origin(k), mine2]
        return remote(part, part, s2_send.at[k - 1], s2_recv.at[k - 1], (g, sib, t))

    def hand(l, e):
        to = r ^ e
        return remote(
            pack.at[l, pl.ds(to * cap, cap)],
            land_ref.at[l, pl.ds(r * cap, cap)],
            hand_send.at[l, e],
            hand_recv.at[l, e],
            (to // DP, to % DP, t),
        )

    def slots(e):
        to = r ^ e
        return remote(
            slot_ref.at[to], slot_out.at[r], slot_send.at[e], slot_recv.at[e], (to // DP, to % DP, t)
        )

    def exchange(n, to):
        pairs = heads // 2
        k = (to - t + T) % T
        i = n * (T - 1) + k - 1
        return remote(
            attn.at[to, pl.ds(n * pairs, pairs)],
            attn_in.at[t, pl.ds(n * pairs, pairs)],
            at_send.at[i],
            at_recv.at[i],
            (g, d, to),
        )

    for k in range(1, T):
        z2(k).start()

    def hello_slots(e, carry):
        slots(e).start()
        return carry

    lax.fori_loop(1, R, hello_slots, 0)
    own_slots = pltpu.make_async_copy(slot_ref.at[r], slot_out.at[r], own_sem.at[layers])
    own_slots.start()

    def own(l):
        span = pl.ds(r * cap, cap)
        return pltpu.make_async_copy(pack.at[l, span], land_ref.at[l, span], own_sem.at[l])

    def hand_over(l):
        takes[l].wait()

        def put(i, carry):
            pack[l, i] = caches[l][order_ref[i]]
            return carry

        lax.fori_loop(0, R * cap, put, 0)

        def send(e, carry):
            hand(l, e).start()
            return carry

        lax.fori_loop(1, R, send, 0)
        own(l).start()

    hand_over(0)

    for c in weights:
        c.wait()
    low = lax.broadcasted_iota(jnp.int32, (rows, lanes), 1) < HD

    gains = gain_ref[...].astype(jnp.float32)
    gain = jnp.concatenate([gains[i : i + 1] for i in range(gains.shape[0])], axis=1)

    def project(p, carry):
        take_tokens(p).wait()
        x = tok[p].astype(jnp.float32)
        inv = lax.rsqrt(jnp.mean(x * x, axis=-1, keepdims=True) + EPS)
        normed = (x * inv * gain).astype(jnp.bfloat16)
        kv = jnp.dot(normed, wkv[...], preferred_element_type=jnp.float32).astype(jnp.bfloat16)
        kvb[pl.ds(per_dev + 2 * p, 2)] = kv.reshape(2, rows // 2, lanes)
        q = jnp.dot(normed, wq[...], preferred_element_type=jnp.float32) * (1.0 / HD**0.5)
        for pair in range(q.shape[1] // lanes):
            both = q[:, pair * lanes : (pair + 1) * lanes]
            n, at = (2 * pair) // heads, (2 * pair) % heads
            q_ref[n, p, at * rows : (at + 1) * rows] = jnp.where(low, both, 0.0).astype(jnp.bfloat16)
            q_ref[n, p, (at + 1) * rows : (at + 2) * rows] = jnp.where(
                low, pltpu.roll(both, HD, 1), 0.0
            ).astype(jnp.bfloat16)
        return carry

    lax.fori_loop(0, prompts, project, 0)
    pl.when(t < T - 1)(lambda: z1(True).start())
    pl.when(t > 0)(lambda: z1(False).start())
    for l in range(1, layers - 2):
        hand_over(l)

    trans = (((1,), (1,)), ((), ()))
    block_len = kvb.shape[1]
    keys = 2 * block_len
    window = per_dev // prompts * block_len
    acc_ref[0] = jnp.zeros(acc_ref.shape[1:], acc_ref.dtype)
    max_ref[0] = jnp.full(max_ref.shape[1:], NEG, max_ref.dtype)
    sum_ref[0] = jnp.zeros(sum_ref.shape[1:], sum_ref.dtype)

    def pair(i):
        return jnp.concatenate([kvb[plan_ref[KEY0, i]], kvb[plan_ref[KEY1, i]]], axis=0)

    def place(i, key):
        return jnp.where(key < block_len, plan_ref[POS0, i] + key, plan_ref[POS1, i] + (key - block_len))

    def seen(i, at, query):
        oldest = -len_ref[0, plan_ref[PROMPT, i]]
        return (at <= query) & (at >= jnp.maximum(query + (1 - window), oldest))

    down = lax.broadcasted_iota(jnp.int32, (keys, 1), 0)
    across = lax.broadcasted_iota(jnp.int32, (1, keys), 1)
    query_down = lax.broadcasted_iota(jnp.int32, (rows, 1), 0)
    query_across = lax.broadcasted_iota(jnp.int32, (1, rows), 1)

    def measure(n, begin, end):
        def step(i, carry):
            p = plan_ref[PROMPT, i]
            kv = pair(i)
            visible = seen(i, place(i, down), query_across)
            first = plan_ref[FIRST, i] == 1
            for h in range(heads):
                q = q_ref[n, p, h * rows : (h + 1) * rows]
                s = lax.dot_general(kv, q, trans, preferred_element_type=jnp.float32)
                s = jnp.where(visible, s, NEG).reshape(keys // 8, 8, rows)
                before = jnp.where(first, NEG, max_ref[i, h])
                m = jnp.maximum(before, jnp.max(s, axis=0))
                total = jnp.sum(jnp.exp(s - m[None]), axis=0)
                sum_ref[i + 1, h] = sum_ref[i, h] * jnp.exp(before - m) + total
                max_ref[i + 1, h] = m
            return carry

        def two(j, carry):
            step(begin + 2 * j, carry)
            return step(begin + 2 * j + 1, carry)

        lax.fori_loop(0, (end - begin) // 2, two, 0)

    def stand(x):
        return jnp.broadcast_to(x, (lanes, rows)).T

    def settle():
        def one(p, carry):
            end = plan_ref[LAST, p] + 1
            for h in range(heads):
                m8 = max_ref[end, h]
                m = jnp.max(m8, axis=0, keepdims=True)
                total = jnp.sum(sum_ref[end, h] * jnp.exp(m8 - m), axis=0, keepdims=True)
                stat_ref[0, p, h] = stand(m)
                stat_ref[1, p, h] = stand(1.0 / total)
            return carry

        lax.fori_loop(0, prompts, one, 0)

    def weigh(n, begin, end):
        def step(i, carry):
            p = plan_ref[PROMPT, i]
            kv = pair(i)
            visible = seen(i, place(i, across), query_down)
            keep = jnp.where(plan_ref[FIRST, i] == 1, 0.0, 1.0)
            for h in range(heads):
                q = q_ref[n, p, h * rows : (h + 1) * rows]
                s = lax.dot_general(q, kv, trans, preferred_element_type=jnp.float32)
                s = jnp.where(visible, s, NEG)
                m, inv = stat_ref[0, p, h], stat_ref[1, p, h]
                e = jnp.exp(s - jnp.concatenate([m, m], axis=1))
                w = (e * jnp.concatenate([inv, inv], axis=1)).astype(jnp.bfloat16)
                o = jnp.dot(w, kv, preferred_element_type=jnp.float32)
                acc_ref[i + 1, h] = acc_ref[i, h] * keep + o
            return carry

        def two(j, carry):
            step(begin + 2 * j, carry)
            return step(begin + 2 * j + 1, carry)

        lax.fori_loop(0, (end - begin) // 2, two, 0)

    def finish(n, j):
        p = turn_of(j, t, T)
        live = lax.broadcasted_iota(jnp.int32, (rows, lanes), 0) < len_ref[1, p]
        end = plan_ref[LAST, p] + 1
        for i in range(heads // 2):
            even, odd = acc_ref[end, 2 * i], acc_ref[end, 2 * i + 1]
            both = jnp.where(live, jnp.where(low, pltpu.roll(even, HD, 1), odd), 0.0)
            attn[p, n * (heads // 2) + i] = both.astype(jnp.bfloat16)
        if j < prompts - 1:
            exchange(n, p).start()

    def plane():
        for k in range(1, T):
            z2(k).wait_recv()
            for e in (1, 2):
                xy(k, e).start()
        hand_over(layers - 2)

    def corner():
        for k in range(1, T):
            for e in (1, 2):
                xy(k, e).wait_recv()
                pass_on(k, e).start()
        hand_over(layers - 1)

    def nothing():
        return None

    turns = (
        (nothing, plane, lambda: line(1), nothing),
        (lambda: line(2), corner, nothing, nothing),
    )
    longest = window // keys + 1
    middle = steps // 4 * 2
    marks = [min(-(-longest * (j + 1) // 2) * 2, steps) for j in range(2)]
    for n in range(groups):
        turn = turns[n] if n < len(turns) else (nothing,) * 4
        measure(n, 0, middle)
        turn[0]()
        measure(n, middle, steps)
        settle()
        turn[1]()
        weigh(n, 0, marks[0])
        finish(n, 0)
        turn[2]()
        weigh(n, marks[0], marks[1])
        finish(n, 1)
        turn[3]()
        weigh(n, marks[1], steps)
        for j in range(2, prompts):
            finish(n, j)

    for k in range(1, T):
        for e in (1, 2):
            across_in(k, e).wait_recv()
        s2(k).start()

    def mix(part, o, begin, last):
        a = jnp.concatenate([part[i] for i in range(part.shape[0])], axis=1)
        w = total_ref.shape[2]

        def tile(j, carry):
            at = pl.ds(pl.multiple_of(j * w, 128), w)
            term = jnp.dot(a, wall[o, :, at], preferred_element_type=jnp.float32)
            total = term if begin else total_ref[j] + term
            if last:
                mixed_ref[:, at] = total.astype(jnp.bfloat16)
            else:
                total_ref[j] = total
            return carry

        lax.fori_loop(0, total_ref.shape[0], tile, 0)

    own_shard.wait()
    mix(attn.at[t], t, True, False)
    outer = (t == 0) | (t == T - 1)
    order = (
        jnp.where(t < T // 2, T - 1, 1),
        jnp.where(outer, 2, jnp.where(t == 1, 1, T - 1)),
        jnp.where(outer, jnp.where(t == 0, 1, T - 1), 2),
    )
    for j, k in enumerate(order):
        if j == T - 2:
            line(T - 1)
        s1(k).wait_recv()
        s2(k).wait_recv()
        for n in range(groups):
            i = n * (T - 1) + k - 1
            part = attn_in.at[origin(k), pl.ds(n * (heads // 2), heads // 2)]
            remote(part, part, at_send.at[i], at_recv.at[i], (g, d, origin(k))).wait_recv()
        mix(attn_in.at[origin(k)], origin(k), False, j == T - 2)

    for k in range(1, T):
        z2(k).wait_send()
        pl.when(passes_on(k))(lambda k=k: forward(k).wait_send())
        s1(k).wait_send()
        s2(k).wait_send()
        for e in (1, 2):
            xy(k, e).wait_send()
            pass_on(k, e).wait_send()
        for n in range(groups):
            exchange(n, (t + k) % T).wait_send()
    pl.when(t < T - 1)(lambda: z1(True).wait_send())
    pl.when(t > 0)(lambda: z1(False).wait_send())
    own_slots.wait()

    def done(e, carry):
        slots(e).wait()
        for l in range(layers):
            hand(l, e).wait()
        return carry

    lax.fori_loop(1, R, done, 0)
    for l in range(layers):
        own(l).wait()


R1_ROWS = 64


def place_kernel(
    slot_ref, land_ref, mixed_ref, out_ref, done_ref, src_ref, zero_ref, held_ref, through_ref, loads, out_sem, last_sem
):
    layers, slots, block_len, _ = out_ref.shape
    total = land_ref.shape[1]
    sources = slot_ref.shape[0]
    cap = total // sources
    first = pltpu.make_async_copy(mixed_ref, through_ref, last_sem)
    last = pltpu.make_async_copy(through_ref, done_ref, last_sem)
    first.start()

    def load(s):
        span = pl.ds(s * cap, cap)
        return pltpu.make_async_copy(land_ref.at[:, span], held_ref.at[:, span], loads.at[s])

    def begin(s, carry):
        load(s).start()
        return carry

    lax.fori_loop(0, sources, begin, 0)
    zero_ref[...] = jnp.zeros_like(zero_ref)

    def clear(j, carry):
        src_ref[j] = -1
        return carry

    lax.fori_loop(0, slots, clear, 0)

    def note(j, carry):
        src_ref[slot_ref[j // cap, j % cap, 0]] = j
        return carry

    lax.fori_loop(0, total, note, 0)

    def fill(j, carry):
        @pl.when(src_ref[j] < 0)
        def _():
            pltpu.make_async_copy(zero_ref, out_ref.at[:, j], out_sem).start()

        return carry

    lax.fori_loop(0, slots, fill, 0)
    first.wait()
    last.start()

    def send(s, carry):
        load(s).wait()
        for k in range(cap):
            slot = slot_ref[s, k, 0]
            pltpu.make_async_copy(
                held_ref.at[:, s * cap + k], out_ref.at[:, slot], out_sem
            ).start()
        return carry

    lax.fori_loop(0, sources, send, 0)

    pltpu.make_async_copy(out_ref, out_ref, out_sem).wait()
    last.wait()


def per_device(tokens, norm_gain, w_query, w_keyval, w_out, kv_cache, lengths, dest_slot):
    prompts = lengths.shape[0]
    all_rows, width = tokens.shape
    rows = all_rows // prompts
    layers, _, blocks_win, block_len, lanes = kv_cache.shape
    per_dev = prompts * blocks_win
    G, DP, T = lax.axis_size("group"), lax.axis_size("dp"), lax.axis_size("tensor")
    R = G * DP
    cap = per_dev // R // 2
    live = R * cap
    steps = -(-(prompts + (live + prompts) // 2) // 2) * 2
    heads = w_query.shape[1] // HD
    groups = heads // GROUP_HEADS
    bf, f32 = jnp.bfloat16, jnp.float32

    smem = pl.BlockSpec(memory_space=pltpu.SMEM)
    hbm = pl.BlockSpec(memory_space=pltpu.HBM)
    vmem = pl.BlockSpec(memory_space=pltpu.VMEM)
    dest_t, len_t = dest_slot.T, lengths.T
    order, plan, slots = pl.pallas_call(
        plan_kernel,
        in_specs=[smem, smem],
        out_specs=[smem, smem, vmem],
        out_shape=[
            jax.ShapeDtypeStruct((live,), jnp.int32),
            jax.ShapeDtypeStruct((7, steps), jnp.int32),
            jax.ShapeDtypeStruct((R, 8, 128), jnp.int32),
        ],
        scratch_shapes=[pltpu.SMEM((R,), jnp.int32)],
        name="plan",
    )(dest_t, len_t)

    sem = pltpu.SemaphoreType.DMA
    depth = w_out.shape[0]
    mixed, landed, slots_in = pl.pallas_call(
        functools.partial(main_kernel, (G, DP, T)),
        in_specs=[smem, smem, smem, vmem, vmem] + [hbm] * 5,
        out_specs=[vmem, hbm, vmem],
        out_shape=[
            jax.ShapeDtypeStruct((rows, width), bf),
            jax.ShapeDtypeStruct((layers, live, block_len, lanes), bf),
            jax.ShapeDtypeStruct((R, 8, 128), jnp.int32),
        ],
        scratch_shapes=[
            pltpu.VMEM((prompts, rows, width), bf),
            pltpu.VMEM(w_query.shape, bf),
            pltpu.VMEM(w_keyval.shape, bf),
            pltpu.VMEM((per_dev + 2 * prompts, block_len, lanes), bf),
            *[pltpu.VMEM((per_dev, block_len, lanes), bf) for _ in range(layers - 1)],
            pltpu.VMEM((layers, live, block_len, lanes), bf),
            pltpu.VMEM((T, depth, width), bf),
            pltpu.VMEM((groups, prompts, GROUP_HEADS * rows, lanes), bf),
            pltpu.VMEM((steps + 1, GROUP_HEADS, rows, lanes), f32),
            pltpu.VMEM((steps + 1, GROUP_HEADS, 8, rows), f32),
            pltpu.VMEM((steps + 1, GROUP_HEADS, 8, rows), f32),
            pltpu.VMEM((2, prompts, GROUP_HEADS, rows, lanes), f32),
            pltpu.VMEM((prompts, heads // 2, rows, lanes), bf),
            pltpu.VMEM((T, heads // 2, rows, lanes), bf),
            pltpu.VMEM((4, rows, width // 4), f32),
            sem((layers + 3 + prompts,)),
            sem((layers + 1,)),
            sem((T + 1,)),
            sem((T - 1,)),
            sem((T - 1,)),
            sem((T - 1,)),
            sem(((T - 1) * 2,)),
            sem(((T - 1) * 2,)),
            sem(((T - 1) * 2,)),
            sem(((T - 1) * 2,)),
            sem((T - 1,)),
            sem((T - 1,)),
            sem((T - 1,)),
            sem((T - 1,)),
            sem((layers, R)),
            sem((layers, R)),
            sem((R,)),
            sem((R,)),
            sem((groups * (T - 1),)),
            sem((groups * (T - 1),)),
        ],
        compiler_params=pltpu.CompilerParams(
            collective_id=0, has_side_effects=True, vmem_limit_bytes=VMEM_LIMIT
        ),
        name="main",
    )(
        order,
        plan,
        len_t,
        slots,
        norm_gain.reshape(-1, lanes),
        tokens.reshape(prompts, rows, width),
        w_query,
        w_keyval,
        w_out,
        kv_cache.reshape(layers, per_dev, block_len, lanes),
    )

    decode_cache, mixed = pl.pallas_call(
        place_kernel,
        in_specs=[smem, hbm, hbm],
        out_specs=[hbm, hbm],
        out_shape=[
            jax.ShapeDtypeStruct((layers, per_dev, block_len, lanes), bf),
            jax.ShapeDtypeStruct((rows, width), bf),
        ],
        scratch_shapes=[
            pltpu.SMEM((per_dev,), jnp.int32),
            pltpu.VMEM((layers, block_len, lanes), bf),
            pltpu.VMEM((layers, live, block_len, lanes), bf),
            pltpu.VMEM((rows, width), bf),
            sem((R,)),
            sem,
            sem,
        ],
        compiler_params=pltpu.CompilerParams(vmem_limit_bytes=VMEM_LIMIT),
        name="place",
    )(slots_in, landed, mixed)
    return (mixed, decode_cache)


def solution(mesh):
    in_specs = (
        P(("group", "dp"), None),
        P(),
        P(None, "tensor"),
        P(None, "tensor"),
        P("tensor", None),
        P(None, ("group", "dp"), None, None, "tensor"),
        P(("group", "dp"), None),
        P(),
    )
    out_specs = (P(("group", "dp", "tensor"), None), P(None, ("group", "dp"), None, "tensor"))
    return jax.shard_map(
        per_device, mesh=mesh, in_specs=in_specs, out_specs=out_specs, check_vma=False
    )
```
